128 devices in a mesh: mem: 4 (over x_hi, core), tile: 32 (over x_lo, y, z).
Axes of the slice: x: 4 (x_hi: 2, x_lo: 2; x = x_hi * 2 + x_lo), y: 4, z: 4, core: 2. Of those that a mesh axis runs over, the one named last changes fastest.
Arguments:
- latents: float32 [24, 256], P('mem'), may hold values from -6 to 6
- basis: bfloat16 [256, 2, 512, 512], P(None, None, 'tile'), may hold values from -0.375 to 0.375
- conv_in: bfloat16 [9, 64], replicated, may hold values from -2 to 2
- conv_mid: bfloat16 [9, 64, 64], replicated, may hold values from -0.25 to 0.25
- conv_out: bfloat16 [64], replicated, may hold values from -0.75 to 0.75
- pressure_prev: float32 [2, 512, 512], P(None, 'tile'), may hold values from -6 to 6
- source: float32 [2, 512, 512], P(None, 'tile'), may hold values from -6 to 6
- perf_cells: int32 [384, 8], replicated, may hold values from 0 to 524287
- perf_count: int32 [384], replicated, may hold values from 1 to 8
- obs_perturbed: float32 [24, 384], replicated, may hold values from -6 to 6
- obs_error: float32 [384], replicated, may hold values from 0.2 to 2
Outputs:
- pressure: float32 [24, 2, 512, 512], P(None, None, 'tile', 'mem')
- well_data: float32 [24, 384], replicated
- latents_new: float32 [24, 256], P('mem')
The draws below stay inside these ranges and needn't reach their ends.
All inputs are finite; a program needn't handle non-finite values.
Results may differ from the reference program's by a relative error of at most 0.0055.
Values may be sent and summed in bfloat16 or wider, within the bound.
A program may use at most 128 MiB of HBM per device.

```python
import math
import jax
import jax.numpy as jnp
from jax import lax

NZ = 2
L = 256
C = 64
WELLS = 384
PERF = 8
SWEEPS = 2
MEMBERS = 24
NX = 512
NY = 512


def with_ends(array, stream_key, least, largest):
    shape = array.shape
    place = [jax.random.randint(jax.random.fold_in(stream_key, axis), (), 0, shape[axis]) for axis in range(len(shape))]
    array = array.at[tuple(place)].set(least)
    longest = shape.index(max(shape))
    place[longest] = (place[longest] + 1) % shape[longest]
    return array.at[tuple(place)].set(largest)


def level_of(key, extent, shards, smallest, top_value):
    level, own = 1.0, jax.random.fold_in(key, 6)
    for dim, shards_of in shards:
        draws = jnp.exp(jax.random.uniform(jax.random.fold_in(own, dim), (shards_of,), jnp.float32, smallest / len(shards), top_value / len(shards)))
        level = level * jnp.repeat(draws, extent[dim] // shards_of).reshape([-1 if axis == dim else 1 for axis in range(len(extent))])
    return level


def noise(stream_key, dims, scale, limit, cuts=(), held_as=jnp.bfloat16):
    result = jax.random.normal(stream_key, dims, jnp.float32) * scale
    if len(cuts) > 0:
        result = level_of(stream_key, dims, cuts, -0.22, 0.18) * result
    return jnp.clip(result, min=-limit, max=limit).astype(held_as)


def setup_inputs(seed: int = 0) -> dict:
    streams_of = jax.random.split(jax.random.key(seed), 12)
    latents = noise(streams_of[0], (MEMBERS, L), 1.0, 6.0, ((0, 4),), jnp.float32)
    basis = noise(streams_of[1], (L, NZ, NX, NY), L ** -0.5, 0.375, ((2, 32),))
    conv_in = noise(streams_of[2], (9, C), 9 ** -0.5, 2.0)
    conv_mid = noise(streams_of[3], (9, C, C), (9 * C) ** -0.5, 0.25)
    conv_out = noise(streams_of[4], (C,), C ** -0.5, 0.75)
    pressure_prev = noise(streams_of[5], (NZ, NX, NY), 1.0, 6.0, ((1, 32),), jnp.float32)
    source = noise(streams_of[6], (NZ, NX, NY), 1.0, 6.0, ((1, 32),), jnp.float32)
    perf_cells = with_ends(jax.random.randint(streams_of[7], (WELLS, PERF), 0, NZ * NX * NY), jax.random.fold_in(streams_of[7], 1), 0, (NZ * NX * NY) - 1).astype(jnp.int32)
    perf_count = with_ends(jax.random.randint(streams_of[8], (WELLS,), 1, PERF + 1), jax.random.fold_in(streams_of[8], 1), 1, PERF).astype(jnp.int32)
    obs_perturbed = noise(streams_of[9], (MEMBERS, WELLS), 1.0, 6.0, (), jnp.float32)
    obs_error = jnp.clip(jnp.exp(jax.random.uniform(streams_of[10], (WELLS,), jnp.float32, math.log(0.2), math.log(2.0))), 0.2, 2.0)
    return dict(latents=latents, basis=basis, conv_in=conv_in, conv_mid=conv_mid, conv_out=conv_out, pressure_prev=pressure_prev, source=source, perf_cells=perf_cells, perf_count=perf_count, obs_perturbed=obs_perturbed, obs_error=obs_error)


storage_coef = 1.0

def lift(field, conv_in):
    rows = field.shape[1] - 2
    width = field.shape[2]
    padded = jnp.pad(field, ((0, 0), (0, 0), (1, 1)))
    total = jnp.zeros((field.shape[0], conv_in.shape[1], rows, width), jnp.float32)
    for tap in range(9):
        part = padded[:, tap // 3:tap // 3 + rows, tap % 3:tap % 3 + width]
        total = total + conv_in[tap].astype(jnp.float32)[None, :, None, None] * part[:, None]
    return jax.nn.relu(total).astype(jnp.bfloat16)

def mix(lifted, field, conv_mid, conv_out):
    rows = field.shape[1]
    width = field.shape[2]
    padded = jnp.pad(lifted.astype(jnp.float32), ((0, 0), (0, 0), (0, 0), (1, 1)))
    total = jnp.zeros((field.shape[0], conv_mid.shape[1], rows, width), jnp.float32)
    for tap in range(9):
        part = padded[:, :, tap // 3:tap // 3 + rows, tap % 3:tap % 3 + width]
        total = total + jnp.einsum('oc,zcxy->zoxy', conv_mid[tap].astype(jnp.float32), part)
    deep = jax.nn.relu(total)
    return field + jnp.einsum('c,zcxy->zxy', conv_out.astype(jnp.float32), deep)

def neighbours(wide):
    zpad = jnp.pad(wide, ((0, 0), (1, 1), (0, 0), (0, 0)))
    return [zpad[:, 1:-1, 2:, 1:-1], zpad[:, 1:-1, :-2, 1:-1], zpad[:, 1:-1, 1:-1, 2:], zpad[:, 1:-1, 1:-1, :-2], zpad[:, 2:, 1:-1, 1:-1], zpad[:, :-2, 1:-1, 1:-1]]

def widen(values):
    return jnp.pad(values, ((0, 0), (0, 0), (1, 1), (1, 1)))

def reference(latents, basis, conv_in, conv_mid, conv_out, pressure_prev, source, perf_cells, perf_count, obs_perturbed, obs_error):
    flat_basis = basis.reshape(basis.shape[0], -1)
    field = jnp.dot(latents.astype(jnp.bfloat16).astype(jnp.float32), flat_basis.astype(jnp.float32), preferred_element_type=jnp.float32)
    field = field.reshape(MEMBERS, NZ, NX, NY)

    def decode(single):
        wide = jnp.pad(single, ((0, 0), (1, 1), (0, 0)))
        lifted = lift(wide, conv_in)
        lifted_wide = jnp.pad(lifted, ((0, 0), (0, 0), (1, 1), (0, 0)))
        return mix(lifted_wide, single, conv_mid, conv_out)
    log_perm = lax.map(decode, field)
    perm = jnp.exp(log_perm)
    conduct = [2.0 * perm * other / (perm + other) for other in neighbours(widen(perm))]
    denom = storage_coef + sum(conduct)
    base = storage_coef * pressure_prev + source
    press = jnp.broadcast_to(pressure_prev, perm.shape).astype(jnp.float32)
    for sweep in range(SWEEPS):
        near = neighbours(widen(press))
        acc = base[None] + sum((cval * nval for cval, nval in zip(conduct, near)))
        press = acc / denom
    ids = perf_cells.reshape(-1).astype(jnp.int32)
    perm_at = jnp.take(perm.reshape(MEMBERS, -1), ids, axis=1).reshape(MEMBERS, WELLS, PERF)
    press_at = jnp.take(press.reshape(MEMBERS, -1), ids, axis=1).reshape(MEMBERS, WELLS, PERF)
    used = (jnp.arange(PERF)[None, :] < perf_count[:, None]).astype(jnp.float32)
    numer = lax.optimization_barrier(jnp.sum(perm_at * press_at * used[None], axis=2))
    weight_sum = lax.optimization_barrier(jnp.sum(perm_at * used[None], axis=2))
    well_data = numer / weight_sum
    scale = 2.0 * obs_error
    centred = well_data - lax.optimization_barrier(jnp.mean(well_data, axis=0, keepdims=True))
    scaled = centred / (math.sqrt(MEMBERS - 1) * scale[None, :])
    innov = (obs_perturbed - well_data) / scale[None, :]
    gram = jnp.eye(MEMBERS, dtype=jnp.float32) + jnp.dot(scaled, scaled.T, precision=lax.Precision.HIGHEST)
    cross = jnp.dot(scaled, innov.T, precision=lax.Precision.HIGHEST)
    factor = jnp.linalg.cholesky(gram)
    weights = jax.scipy.linalg.cho_solve((factor, True), cross)
    spread = (latents - lax.optimization_barrier(jnp.mean(latents, axis=0, keepdims=True))) / math.sqrt(MEMBERS - 1)
    latents_new = latents + jnp.dot(weights.T, spread, precision=lax.Precision.HIGHEST)
    return (press, well_data, latents_new)
```

```python
import math

import jax
import jax.numpy as jnp
from jax import lax
from jax.experimental import pallas as pl
from jax.experimental.pallas import tpu as pltpu
from jax.sharding import PartitionSpec as P

SWEEPS = 2
STORAGE = 1.0
BF = jnp.bfloat16
F32 = jnp.float32
LANES = 128
HALO = 4
WINDOW = 32
PER_WINDOW = (WINDOW - 2) // 2
MESH = pl.DeviceIdType.MESH
BIG = 60 * 2**20


def dot(a, b):
    return jnp.dot(a, b, preferred_element_type=F32)


def dot_nt(a, b, precision=None):
    return lax.dot_general(a, b, (((1,), (1,)), ((), ())), preferred_element_type=F32, precision=precision)


def iota(shape, axis):
    return lax.broadcasted_iota(jnp.int32, shape, axis)


def ones_where(cond):
    return jnp.where(cond, 1.0, 0.0)


def field_kernel(
    lat_ref, basis_ref, prev_ref, source_ref, own_ref, halo_ref, edge_ref, every_ref,
    gathered, slab, left, send, edge_send, lat_sems, row_sems, slab_sems,
):
    mem = lax.axis_index("mem")
    tile = lax.axis_index("tile")
    mems = lax.axis_size("mem")
    tiles = lax.axis_size("tile")
    share, latent = lat_ref.shape
    members = share * mems
    rows = own_ref.shape[0]
    layers = basis_ref.shape[1]
    before, after = lax.rem(tile + tiles - 1, tiles), lax.rem(tile + 1, tiles)

    loads = []
    for part, offset in enumerate((0, -1, 1)):
        at = jnp.clip(mem + offset, 0, mems - 1)
        loads.append(
            pltpu.make_async_copy(
                basis_ref.at[:, :, :, pl.ds(pl.multiple_of(at * LANES, LANES), LANES)],
                slab.at[part],
                slab_sems.at[part],
            )
        )
    for load in loads:
        load.start()

    barrier = pltpu.get_barrier_semaphore()
    for step in range(1, mems):
        pl.semaphore_signal(barrier, inc=1, device_id={"mem": lax.rem(mem + step, mems)}, device_id_type=MESH)
    for other in (before, after):
        pl.semaphore_signal(barrier, inc=1, device_id={"tile": other}, device_id_type=MESH)
    pl.semaphore_wait(barrier, mems + 1)

    copies = []
    for step in range(1, mems):
        copies.append(
            pltpu.make_async_remote_copy(
                src_ref=lat_ref,
                dst_ref=gathered.at[mem],
                send_sem=lat_sems.at[0, step],
                recv_sem=lat_sems.at[1, step],
                device_id={"mem": lax.rem(mem + step, mems)},
                device_id_type=MESH,
            )
        )
        copies[-1].start()

    for side in range(2):
        first = 0 if side == 0 else rows - 2
        edge = 0 if side == 0 else rows - 1
        for z in range(layers):
            edge_send[side, 2 * z : 2 * z + 2] = prev_ref[z, first : first + 2]
            edge_send[side, 4 + z : 5 + z] = source_ref[z, edge : edge + 1]
        edge_send[side, 6:8] = jnp.zeros_like(edge_send[side, 6:8])
    row_copies = []
    for side, other in ((0, before), (1, after)):
        row_copies.append(
            pltpu.make_async_remote_copy(
                src_ref=edge_send.at[side],
                dst_ref=edge_ref.at[1 - side],
                send_sem=row_sems.at[0, side],
                recv_sem=row_sems.at[1, side],
                device_id={"tile": other},
                device_id_type=MESH,
            )
        )
        row_copies[-1].start()

    gathered[mem] = lat_ref[...]
    for copy in copies:
        copy.wait()
    for s in range(mems):
        every_ref[share * s : share * (s + 1)] = gathered[s]
    every = every_ref[...].astype(BF).astype(F32)

    groups = latent // rows
    wide = rows * rows
    group_of = iota((1, latent), 1) // rows
    picked = jnp.concatenate([every * ones_where(group_of == g) for g in range(groups)], axis=0).astype(BF)
    spread = ones_where(lax.rem(iota((latent, wide), 0), rows) == iota((latent, wide), 1) // rows).astype(BF)
    repeated = dot(picked, spread)
    lane_row = lax.rem(iota((1, wide), 1), rows)
    for g in range(groups):
        part = repeated[g * members : (g + 1) * members]
        stacked = jnp.concatenate([part * ones_where(lane_row == r) for r in range(rows)], axis=0)
        left[:, g * wide : (g + 1) * wide] = stacked.astype(BF)
    for load in loads:
        load.wait()
    lane = iota((1, LANES), 1)
    keep_left = (ones_where(lane >= LANES // 2) * jnp.where(mem > 0, 1.0, 0.0)).astype(BF)
    keep_right = (ones_where(lane < LANES // 2) * jnp.where(mem < mems - 1, 1.0, 0.0)).astype(BF)
    for z in range(layers):
        own = slab[0, :, z].reshape(latent * rows, LANES)
        lhs = slab[1, :, z].reshape(latent * rows, LANES)
        rhs = slab[2, :, z].reshape(latent * rows, LANES)
        both = jnp.concatenate([own, lhs * keep_left + rhs * keep_right], axis=1)
        field = dot(left[...], both).reshape(rows, members, 2 * LANES)
        own_ref[:, z * members : (z + 1) * members] = field
    send[0:HALO] = own_ref[0:HALO].astype(BF)
    send[HALO : 2 * HALO] = own_ref[rows - HALO : rows].astype(BF)
    for side, other in ((0, before), (1, after)):
        row_copies.append(
            pltpu.make_async_remote_copy(
                src_ref=send.at[pl.ds(side * HALO, HALO)],
                dst_ref=halo_ref.at[pl.ds((1 - side) * HALO, HALO)],
                send_sem=row_sems.at[0, 2 + side],
                recv_sem=row_sems.at[1, 2 + side],
                device_id={"tile": other},
                device_id_type=MESH,
            )
        )
        row_copies[-1].start()
    for copy in row_copies:
        copy.wait()


def fields(latents, basis, prev, source):
    share, latent = latents.shape
    mems = lax.axis_size("mem")
    members = share * mems
    _, layers, rows, width = basis.shape
    vmem = pl.BlockSpec(memory_space=pltpu.VMEM)
    return pl.pallas_call(
        field_kernel,
        out_shape=[
            jax.ShapeDtypeStruct((rows, layers * members, 2 * LANES), F32),
            jax.ShapeDtypeStruct((2 * HALO, layers * members, 2 * LANES), BF),
            jax.ShapeDtypeStruct((2, 8, width), F32),
            jax.ShapeDtypeStruct((members, latent), F32),
        ],
        in_specs=[vmem, pl.BlockSpec(memory_space=pl.ANY), vmem, vmem],
        out_specs=[vmem] * 4,
        scratch_shapes=[
            pltpu.VMEM((mems, share, latent), F32),
            pltpu.VMEM((3, latent, layers, rows, LANES), BF),
            pltpu.VMEM((rows * members, latent * rows), BF),
            pltpu.VMEM((2 * HALO, layers * members, 2 * LANES), BF),
            pltpu.VMEM((2, 8, width), F32),
            pltpu.SemaphoreType.DMA((2, mems)),
            pltpu.SemaphoreType.DMA((2, 4)),
            pltpu.SemaphoreType.DMA((3,)),
        ],
        compiler_params=pltpu.CompilerParams(collective_id=0, has_side_effects=True, vmem_limit_bytes=BIG),
        name="fields",
    )(latents, basis, prev, source)


def decoder_weights(conv_in_ref, conv_mid_ref, conv_out_ref, taps, lift_w, mix_w, out_w, mem, mems, last):
    channels = conv_out_ref.shape[1]
    block = 4 * channels
    taps[...] = jnp.zeros_like(taps)
    taps[0:9] = conv_in_ref[...].astype(F32)
    repeat = ones_where(iota((channels, block), 0) == lax.rem(iota((channels, block), 1), channels)).astype(BF)
    in_rows = dot(taps[...].astype(BF), repeat)
    in_rows = jnp.concatenate([in_rows] * 4, axis=0)
    in_rows = (in_rows * ones_where(iota((64, block), 0) // 16 == iota((64, block), 1) // channels)).astype(BF)
    row = iota((block, 64), 0)
    col = iota((block, 64), 1)
    column = lax.rem(row, WINDOW)
    patch_row = lax.rem(row // WINDOW, 4)
    tap = lax.rem(col, 16)
    tap_row = jnp.where(tap >= 3, 1, 0) + jnp.where(tap >= 6, 1, 0)
    tap_col = tap - 3 * tap_row
    fits = (patch_row == col // 32 + tap_row) & (tap < 9)
    offset = jnp.where(fits, column - lax.rem(col // 16, 2) - tap_col, -1)
    col_of = lax.rem(iota((1, block), 1) // channels, 2)
    low, high = jnp.where(mem > 0, 1.0, 0.0), jnp.where(mem < mems - 1, 1.0, 0.0)
    for t in range(PER_WINDOW):
        weight = dot(ones_where(offset == 2 * t).astype(BF), in_rows)
        lift_w[t] = weight.astype(BF)
        if t == 0:
            lift_w[PER_WINDOW] = (weight * low).astype(BF)
        if t == 1:
            lift_w[PER_WINDOW + 1] = (weight * jnp.where(col_of == 0, low, 1.0)).astype(BF)
        if t == (last - 1) % PER_WINDOW:
            lift_w[PER_WINDOW + 2] = (weight * jnp.where(col_of == 1, high, 1.0)).astype(BF)
        if t == last % PER_WINDOW:
            lift_w[PER_WINDOW + 3] = (weight * high).astype(BF)
    mix_w[...] = jnp.zeros_like(mix_w)
    nothing = jnp.zeros((channels, channels), F32)
    for p in range(4):
        for q in range(4):
            at = ((q // 2) * 2 + p // 2) * block + ((p % 2) * 2 + q % 2) * channels
            for a in range(2):
                if not 0 <= p - a <= 2:
                    continue
                pair = [
                    conv_mid_ref[3 * (p - a) + q - b].astype(F32) if 0 <= q - b <= 2 else nothing for b in range(2)
                ]
                mix_w[at : at + channels, a * 2 * channels : (a + 1) * 2 * channels] = (
                    jnp.concatenate(pair, axis=0).T.astype(BF)
                )
    out_row = conv_out_ref[...].astype(F32)
    diag = iota((channels, channels), 0) == iota((channels, channels), 1)
    out_col = jnp.sum(jnp.where(diag, out_row, 0.0), axis=1, keepdims=True)
    out_col = jnp.concatenate([out_col] * 4, axis=0)
    group = iota((block, 2 * LANES), 0) // channels
    lane = iota((block, 2 * LANES), 1)
    match = (group // 2 == lane // LANES) & (lax.rem(group, 2) == lax.rem(lane, 2))
    out_w[...] = jnp.where(match, out_col, 0.0).astype(BF)


def field_windows(own_ref, halo_ref, windows, pieces, tile, tiles):
    rows = own_ref.shape[0]
    lane = iota((1, LANES), 1)
    top = jnp.where(tile > 0, 1.0, 0.0)
    bottom = jnp.where(tile < tiles - 1, 1.0, 0.0)
    count = windows.shape[0]

    def row_pieces(field, odd):
        own, halo = field[:, :LANES], field[:, LANES:]
        low = jnp.where(lane < LANES // 2, own, halo)
        high = jnp.where(lane < LANES // 2, halo, own)
        out = []
        for w in range(count):
            start = (WINDOW - 2) * w - HALO
            from_tile = low if w == 0 else high if w == count - 1 else own
            out.append(pltpu.roll(from_tile, (WINDOW * odd - start) % LANES, 1))
        return out

    def pair_pieces(q, even, odd):
        evens, odds = row_pieces(even, 0), row_pieces(odd, 1)
        for w in range(count):
            pieces[q, w] = jnp.where(lane < WINDOW, evens[w], odds[w])

    for half in range(HALO // 2):
        pair_pieces(half, halo_ref[2 * half].astype(F32) * top, halo_ref[2 * half + 1].astype(F32) * top)
        at = HALO + 2 * half
        pair_pieces(
            (rows + at) // 2, halo_ref[at].astype(F32) * bottom, halo_ref[at + 1].astype(F32) * bottom
        )

    def own_pair(q, carry):
        pair_pieces(q + HALO // 2, own_ref[2 * q], own_ref[2 * q + 1])
        return carry

    lax.fori_loop(0, rows // 2, own_pair, 0)
    members = own_ref.shape[1]

    def block_row(i, carry):
        for w in range(count):
            both = jnp.where(lane < LANES // 2, pieces[i, w], pltpu.roll(pieces[i + 1, w], LANES // 2, 1))
            high = both.astype(BF)
            windows[w, i] = jnp.concatenate([high, (both - high.astype(F32)).astype(BF)], axis=1)
        return carry

    lax.fori_loop(0, windows.shape[1], block_row, 0)


def convolve(windows, lift_w, mix_w, out_w, lifted, mixed, total, ends, tile, tiles, blocks):
    count, block_rows, deep, _ = windows.shape
    size = (block_rows - 1) * deep
    lane = iota((1, 2 * LANES), 1)
    pair = lax.rem(lane, LANES) // 2
    part = lane // LANES
    top = jnp.where(tile > 0, 1.0, 0.0)
    bottom = jnp.where(tile < tiles - 1, 1.0, 0.0)
    masks = {
        0: jnp.zeros((1, 2 * LANES), F32) + top,
        1: jnp.where(part == 0, top, 1.0),
        block_rows - 2: jnp.where(part == 1, bottom, 1.0),
        block_rows - 1: jnp.zeros((1, 2 * LANES), F32) + bottom,
    }

    def lift(k, slot):
        for u in range(2):
            at = jnp.minimum(2 * k + u, blocks)
            w = at // PER_WINDOW
            index = at - w * PER_WINDOW
            for special, j in enumerate((0, 1, blocks - 1, blocks)):
                index = jnp.where(at == j, PER_WINDOW + special, index)
            value = jnp.maximum(dot(windows[w].reshape(block_rows * deep, -1), lift_w[index]), 0.0)
            parts = [value[i * deep : (i + 1) * deep] for i in range(block_rows)]
            parts = [p * masks[i] if i in masks else p for i, p in enumerate(parts)]
            lifted[slot][u] = jnp.concatenate(parts, axis=0).astype(BF)

    def mix(k, slot, to):
        held = [lifted[slot].at[0], lifted[slot].at[1], lifted[(slot + 1) % 3].at[0]]
        for u in range(2):
            x, y = held[u], held[u + 1]
            lhs = jnp.concatenate([x[0:size], x[deep : deep + size], y[0:size], y[deep : deep + size]], axis=1)
            mixed[to][u] = jnp.maximum(dot(lhs, mix_w[...]), 0.0).astype(BF)

    def contract(k, at, first=False, last=False):
        even = dot(mixed[at][0], out_w[...])
        odd = dot(mixed[at][1], out_w[...])
        j = 2 * k
        if first:
            ends[...] = even
            total[...] = odd
        elif last:
            total[...] = jnp.where(pair == j - 1, even, total[...])
            ends[...] = jnp.where(pair == 0, odd, ends[...])
        else:
            total[...] = jnp.where(pair == j - 1, even, jnp.where(pair == j, odd, total[...]))

    steps = blocks // 2
    lift(0, 0)
    lift(1, 1)
    mix(0, 0, 0)
    lift(2, 2)
    contract(0, 0, first=True)
    mix(1, 1, 1)
    lift(3, 0)

    def body(q, carry):
        for v in range(6):
            k = 2 + q * 6 + v
            contract(k - 1, (1 + v) % 2)
            mix(k, (2 + v) % 3, v % 2)
            lift(k + 2, (4 + v) % 3)
        return carry

    lax.fori_loop(0, (steps - 3) // 6, body, 0)
    k = steps - 1
    contract(k - 1, (k - 1) % 2)
    mix(k, k % 3, k % 2)
    contract(k, k % 2, last=True)


def sweeps(
    own_ref, halo_ref, edge_ref, prev_ref, source_ref, total, ends, perm, first, press_ref, values,
    mem, mems, tile, tiles,
):
    rows = own_ref.shape[0]
    deep = own_ref.shape[1]
    layers = prev_ref.shape[0]
    members = deep // layers
    lane = iota((1, LANES), 1)
    top = jnp.where(tile > 0, 1.0, 0.0)
    bottom = jnp.where(tile < tiles - 1, 1.0, 0.0)
    beyond = jnp.where(lane < LANES // 2, jnp.where(mem < mems - 1, 1.0, 0.0), jnp.where(mem > 0, 1.0, 0.0))
    mine = pl.multiple_of(mem * LANES, LANES)
    before = pl.multiple_of(jnp.maximum(mem - 1, 0) * LANES, LANES)
    after = pl.multiple_of(jnp.minimum(mem + 1, mems - 1) * LANES, LANES)

    def columns(line):
        beside = jnp.where(lane < LANES // 2, line(after), line(before))
        return line(mine), beside

    def levels(pick):
        each = [columns(lambda at: pick(z, at)) for z in range(layers)]
        return [
            jnp.concatenate([jnp.broadcast_to(each[z][t], (members, LANES)) for z in range(layers)], axis=0)
            for t in range(2)
        ]

    def prev_line(index):
        r = index - 2
        if r < 0:
            return levels(lambda z, at: edge_ref[0, 2 * z + 2 + r : 2 * z + 3 + r, pl.ds(at, LANES)])
        if r >= rows:
            return levels(lambda z, at: edge_ref[1, 2 * z + r - rows : 2 * z + r - rows + 1, pl.ds(at, LANES)])
        return levels(lambda z, at: prev_ref[z, r : r + 1, pl.ds(at, LANES)])

    def source_line(index):
        r = index - 2
        if r < 0:
            return levels(lambda z, at: edge_ref[0, 4 + z : 5 + z, pl.ds(at, LANES)])
        if r >= rows:
            return levels(lambda z, at: edge_ref[1, 4 + z : 5 + z, pl.ds(at, LANES)])
        return levels(lambda z, at: source_ref[z, r : r + 1, pl.ds(at, LANES)])

    for index in range(rows + 4):
        r = index - 2
        i, a = index // 2, index % 2
        for t, parts in enumerate((total, ends)):
            value = parts[i * deep : (i + 1) * deep, a * LANES : (a + 1) * LANES]
            if 0 <= r < rows:
                field = own_ref[r, :, t * LANES : (t + 1) * LANES]
            else:
                at = HALO + r if r < 0 else HALO + r - rows
                field = halo_ref[at, :, t * LANES : (t + 1) * LANES].astype(F32)
            value = jnp.exp(field + value)
            if r < 0:
                value = jnp.where(top > 0, value, 0.0)
            if r >= rows:
                value = jnp.where(bottom > 0, value, 0.0)
            if t == 1:
                value = jnp.where(beyond > 0, value, 0.0)
            perm[index, t] = value

    def shift(own, beside, by):
        edge = LANES - 1 if by > 0 else 0
        a, b = pltpu.roll(own, -by % LANES, 1), pltpu.roll(beside, -by % LANES, 1)
        return jnp.where(lane == edge, b, a), jnp.where(lane == edge, a, b)

    def harmonic(a, b):
        both = a + b
        return jnp.where(both > 0, 2.0 * a * b / jnp.where(both > 0, both, 1.0), 0.0)

    def swap(x):
        return jnp.concatenate([x[members:], x[:members]], axis=0)

    def coefficients(index):
        here = [perm[index, t] for t in range(2)]
        right = shift(here[0], here[1], 1)
        across = [harmonic(here[t], right[t]) for t in range(2)]
        back = shift(across[0], across[1], -1)
        out = []
        for t in range(2):
            level = harmonic(here[t][:members], here[t][members:])
            out.append((across[t], back[t], jnp.concatenate([level, level], axis=0)))
        return out

    up = [harmonic(perm[0, t], perm[1, t]) for t in range(2)]
    lines = [prev_line(0), prev_line(1)]
    for index in range(1, rows + 3):
        lines.append(prev_line(index + 1))
        down = [harmonic(perm[index, t], perm[index + 1, t]) for t in range(2)]
        coef = coefficients(index)
        here = lines[index]
        right, back = shift(here[0], here[1], 1), shift(here[0], here[1], -1)
        source = source_line(index)
        for t in range(2):
            east, west, level = coef[t]
            acc = STORAGE * here[t] + source[t]
            acc = acc + down[t] * lines[index + 1][t] + up[t] * lines[index - 1][t]
            acc = acc + east * right[t] + west * back[t] + level * swap(here[t])
            first[index, t] = acc / (STORAGE + down[t] + up[t] + east + west + level)
        up = down
    up = harmonic(perm[1, 0], perm[2, 0])
    for index in range(2, rows + 2):
        r = index - 2
        down = harmonic(perm[index, 0], perm[index + 1, 0])
        east, west, level = coefficients(index)[0]
        here = first[index, 0]
        right = shift(here, first[index, 1], 1)[0]
        back = shift(here, first[index, 1], -1)[0]
        acc = STORAGE * lines[index][0] + source_line(index)[0]
        acc = acc + down * first[index + 1, 0] + up * first[index - 1, 0]
        acc = acc + east * right + west * back + level * swap(here)
        press = acc / (STORAGE + down + up + east + west + level)
        up = down
        k = perm[index, 0]
        for z in range(layers):
            level_press = press[z * members : (z + 1) * members]
            level_perm = k[z * members : (z + 1) * members]
            press_ref[:, z, r, :] = level_press
            at = (z * rows + r) * LANES
            for q, value in enumerate((level_perm, level_perm * level_press)):
                high = value.astype(BF).astype(F32)
                both = jnp.concatenate([high, value - high], axis=0).astype(BF)
                values[2 * q * members : 2 * (q + 1) * members, at : at + LANES] = both


def well_sums(cells_ref, count_ref, values, pick, pieces_ref, mem, tile, grid_cols, grid_cells, rows):
    wells, slots = cells_ref.shape
    groups, members, _ = pieces_ref.shape
    each = wells // groups
    cells = cells_ref[...]
    layer = cells // grid_cells
    rest = cells - layer * grid_cells
    row = rest // grid_cols
    col = rest - row * grid_cols - mem * LANES
    row = row - tile * rows
    square = (iota((wells, wells), 0), iota((wells, wells), 1))
    counts = jnp.sum(jnp.where(square[0] == square[1], count_ref[...].astype(F32), 0.0), axis=1, keepdims=True)
    used = iota((wells, slots), 1).astype(F32) < counts
    inside = (row >= 0) & (row < rows) & (col >= 0) & (col < LANES) & used
    mask = ones_where(inside)
    code = (((layer * rows + row) * LANES + col) * 512 + iota((wells, slots), 0) + 1).astype(F32)
    code = jnp.where(inside, code, 0.0)
    earlier = dot(ones_where(square[1] < square[0]).astype(BF), mask.astype(BF))
    totals = jnp.sum(mask, axis=0, keepdims=True)
    rank = []
    start = jnp.zeros((1, 1), F32)
    for s in range(slots):
        rank.append(jnp.where(inside[:, s : s + 1], earlier[:, s : s + 1] + start, -1.0))
        start = start + totals[:, s : s + 1]
    code = [code[:, s : s + 1] for s in range(slots)]
    chunks = (jnp.sum(mask).astype(jnp.int32) + LANES - 1) // LANES
    pieces_ref[...] = jnp.zeros_like(pieces_ref)
    cells_local = values.shape[1]
    place = lax.rem(iota((groups * LANES, LANES), 0), LANES)
    well_at = iota((groups * LANES, LANES), 0) // LANES * each + place
    number = jnp.where(place < each, well_at, -7)
    weight = jnp.where((place >= each) & (place < 2 * each), well_at - each, -7)

    def chunk(n, carry):
        wanted = (iota((1, LANES), 1) + n * LANES).astype(F32)
        found = jnp.zeros((1, LANES), F32)
        for s in range(slots):
            found = found + jnp.sum(jnp.where(rank[s] == wanted, code[s], 0.0), axis=0, keepdims=True)
        found = found.astype(jnp.int32) - 1
        cell = jnp.where(found >= 0, found // 512, -1)
        well = jnp.where(found >= 0, lax.rem(found, 512), -1)
        pick[...] = ones_where(iota((cells_local, LANES), 0) == cell).astype(BF)
        got = dot(values[...], pick[...])
        for q, (target, name) in enumerate(((weight, "w"), (number, "n"))):
            sums = got[2 * q * members : (2 * q + 1) * members] + got[(2 * q + 1) * members : (2 * q + 2) * members]
            high = sums.astype(BF).astype(F32)
            both = jnp.concatenate([high, sums - high], axis=0).astype(BF)
            out = dot_nt(both, ones_where(target == well).astype(BF))
            out = out[:members] + out[members:]
            for g in range(groups):
                pieces_ref[g] += out[:, g * LANES : (g + 1) * LANES]
        return carry

    lax.fori_loop(0, chunks, chunk, 0)


def cells_kernel(
    own_ref, halo_ref, edge_ref, conv_in_ref, conv_mid_ref, conv_out_ref, prev_ref, source_ref, cells_ref, count_ref,
    press_ref, pieces_ref,
    taps, lift_w, mix_w, out_w, pieces, windows, l0, l1, l2, m0, m1, total, ends, perm, first, values, pick,
):
    mem, mems = lax.axis_index("mem"), lax.axis_size("mem")
    tile, tiles = lax.axis_index("tile"), lax.axis_size("tile")
    rows = own_ref.shape[0]
    blocks = LANES // 2 + 2
    decoder_weights(conv_in_ref, conv_mid_ref, conv_out_ref, taps, lift_w, mix_w, out_w, mem, mems, blocks)
    field_windows(own_ref, halo_ref, windows, pieces, tile, tiles)
    convolve(windows, lift_w, mix_w, out_w, (l0, l1, l2), (m0, m1), total, ends, tile, tiles, blocks)
    sweeps(
        own_ref, halo_ref, edge_ref, prev_ref, source_ref, total, ends, perm, first, press_ref, values,
        mem, mems, tile, tiles,
    )
    grid_cols = prev_ref.shape[2]
    well_sums(
        cells_ref, count_ref, values, pick, pieces_ref, mem, tile, grid_cols, grid_cols * rows * tiles, rows
    )


def cells(own, halo, edge, conv_in, conv_mid, conv_out, prev, source, perf_cells, perf_count, groups):
    rows, deep, _ = own.shape
    layers = prev.shape[0]
    members = deep // layers
    channels = conv_in.shape[1]
    block = 4 * channels
    blocks = LANES // 2 + 2
    count = blocks // PER_WINDOW + 1
    out_rows = rows // 2 + 2
    vmem = pl.BlockSpec(memory_space=pltpu.VMEM)
    return pl.pallas_call(
        cells_kernel,
        out_shape=[
            jax.ShapeDtypeStruct((members, layers, rows, LANES), F32),
            jax.ShapeDtypeStruct((groups, members, LANES), F32),
        ],
        in_specs=[vmem] * 10,
        out_specs=[vmem] * 2,
        scratch_shapes=[
            pltpu.VMEM((16, channels), F32),
            pltpu.VMEM((PER_WINDOW + 4, block, block), BF),
            pltpu.VMEM((4 * block, block), BF),
            pltpu.VMEM((block, 2 * LANES), BF),
            pltpu.VMEM((rows // 2 + HALO, count, deep, LANES), F32),
            pltpu.VMEM((count, out_rows + 1, deep, 2 * LANES), BF),
        ]
        + [pltpu.VMEM((2, (out_rows + 1) * deep, block), BF)] * 3
        + [pltpu.VMEM((2, out_rows * deep, block), BF)] * 2
        + [pltpu.VMEM((out_rows * deep, 2 * LANES), F32)] * 2
        + [pltpu.VMEM((rows + 4, 2, deep, LANES), F32)] * 2
        + [
            pltpu.VMEM((4 * members, layers * rows * LANES), BF),
            pltpu.VMEM((layers * rows * LANES, LANES), BF),
        ],
        compiler_params=pltpu.CompilerParams(vmem_limit_bytes=BIG),
        name="cells",
    )(own, halo, edge, conv_in, conv_mid, conv_out.reshape(1, channels), prev, source, perf_cells,
      perf_count.reshape(1, -1))


def smoother_kernel(
    pieces_ref, every_ref, obs_ref, error_ref, well_ref, new_ref,
    group_in, y_in, z_in, data_in, hold, group_sems, y_sems, z_sems, data_sems,
):
    mem, tile = lax.axis_index("mem"), lax.axis_index("tile")
    mems = lax.axis_size("mem")
    side = y_in.shape[0]
    plane = side * side
    halves = lax.axis_size("tile") // plane
    groups = mems * halves
    x_lo, y, z = tile // plane, lax.rem(tile // side, side), lax.rem(tile, side)
    mine = mem * halves + x_lo
    members = every_ref.shape[0]

    def in_group(g):
        return {"mem": g // halves, "tile": lax.rem(g, halves) * plane + lax.rem(tile, plane)}

    def along_y(at):
        return {"mem": mem, "tile": x_lo * plane + at * side + z}

    def along_z(at):
        return {"mem": mem, "tile": x_lo * plane + y * side + at}

    barrier = pltpu.get_barrier_semaphore()
    for place, at, size in ((in_group, mine, groups), (along_y, y, side), (along_z, z, side)):
        for step in range(1, size):
            pl.semaphore_signal(barrier, inc=1, device_id=place(lax.rem(at + step, size)), device_id_type=MESH)
    pl.semaphore_wait(barrier, groups + 2 * side - 3)

    def exchange(place, at, size, source, target, sems):
        copies = []
        for step in range(1, size):
            to = lax.rem(at + step, size)
            copies.append(
                pltpu.make_async_remote_copy(
                    src_ref=source(to),
                    dst_ref=target.at[at],
                    send_sem=sems.at[0, step],
                    recv_sem=sems.at[1, step],
                    device_id=place(to),
                    device_id_type=MESH,
                )
            )
            copies[-1].start()
        return copies

    def total(target, size):
        value = target[0]
        for at in range(1, size):
            value = value + target[at]
        return value

    copies = exchange(in_group, mine, groups, lambda to: pieces_ref.at[to], group_in, group_sems)
    group_in[mine] = pieces_ref[mine]
    for copy in copies:
        copy.wait()
    for stage, (place, at, target, sems, source) in enumerate(
        ((along_y, y, y_in, y_sems, group_in), (along_z, z, z_in, z_sems, y_in))
    ):
        value = total(source, source.shape[0])
        hold[stage] = value
        target[at] = value
        copies = exchange(place, at, side, lambda to: hold.at[stage], target, sems)
        for copy in copies:
            copy.wait()
    value = total(z_in, side)
    each = obs_ref.shape[1] // groups
    data = value / pltpu.roll(value, LANES - each, 1)
    hold[2] = data
    data_in[mine] = data
    copies = exchange(in_group, mine, groups, lambda to: hold.at[2], data_in, data_sems)
    for copy in copies:
        copy.wait()

    lane = iota((1, LANES), 1)
    parts = []
    for t in range(obs_ref.shape[1] // LANES):
        part = jnp.zeros((members, LANES), F32)
        for g in range(groups):
            by = each * g - LANES * t
            if by <= -each or by >= LANES:
                continue
            moved = pltpu.roll(data_in[g], by % LANES, 1)
            part = jnp.where((lane >= by) & (lane < by + each), moved, part)
        parts.append(part)
    wells = jnp.concatenate(parts, axis=1)
    well_ref[...] = wells
    scale = 2.0 * error_ref[...]
    centred = wells - jnp.sum(wells, axis=0, keepdims=True) / members
    scaled = centred / (math.sqrt(members - 1) * scale)
    innov = (obs_ref[...] - wells) / scale
    exact = lax.Precision.HIGHEST
    eye = ones_where(iota((members, members), 0) == iota((members, members), 1))
    gram = eye + dot_nt(scaled, scaled, exact)
    cross = dot_nt(innov, scaled, exact)
    work = jnp.concatenate([gram, eye], axis=1)
    row_at = iota((members, 1), 0)
    for k in range(members):
        line = work[k : k + 1] / work[k : k + 1, k : k + 1]
        work = jnp.where(row_at == k, line, work - work[:, k : k + 1] * line)
    inverse = work[:, members:]
    weights = jnp.dot(cross, inverse, preferred_element_type=F32, precision=exact)
    every = every_ref[...]
    spread = (every - jnp.sum(every, axis=0, keepdims=True) / members) / math.sqrt(members - 1)
    new = every + jnp.dot(weights, spread, preferred_element_type=F32, precision=exact)
    share = members // mems
    own = new[0:share]
    for s in range(1, mems):
        own = jnp.where(mem == s, new[s * share : (s + 1) * share], own)
    new_ref[...] = own


def smooth(pieces, every, obs, error):
    groups, members, _ = pieces.shape
    mems, tiles = lax.axis_size("mem"), lax.axis_size("tile")
    side = math.isqrt(tiles * mems // groups)
    vmem = pl.BlockSpec(memory_space=pltpu.VMEM)
    return pl.pallas_call(
        smoother_kernel,
        out_shape=[
            jax.ShapeDtypeStruct(obs.shape, F32),
            jax.ShapeDtypeStruct((members // mems, every.shape[1]), F32),
        ],
        in_specs=[vmem] * 4,
        out_specs=[vmem] * 2,
        scratch_shapes=[
            pltpu.VMEM((groups, members, LANES), F32),
            pltpu.VMEM((side, members, LANES), F32),
            pltpu.VMEM((side, members, LANES), F32),
            pltpu.VMEM((groups, members, LANES), F32),
            pltpu.VMEM((3, members, LANES), F32),
            pltpu.SemaphoreType.DMA((2, groups)),
            pltpu.SemaphoreType.DMA((2, side)),
            pltpu.SemaphoreType.DMA((2, side)),
            pltpu.SemaphoreType.DMA((2, groups)),
        ],
        compiler_params=pltpu.CompilerParams(collective_id=1, has_side_effects=True, vmem_limit_bytes=BIG),
        name="smoother",
    )(pieces, every, obs, error.reshape(1, -1))


def body(
    latents, basis, conv_in, conv_mid, conv_out, pressure_prev, source, perf_cells, perf_count, obs_perturbed, obs_error
):
    groups = 2 * lax.axis_size("mem")
    own, halo, edge, every = fields(latents, basis, pressure_prev, source)
    press, pieces = cells(
        own, halo, edge, conv_in, conv_mid, conv_out, pressure_prev, source, perf_cells, perf_count, groups
    )
    well_data, latents_new = smooth(pieces, every, obs_perturbed, obs_error)
    return press, well_data, latents_new


def solution(mesh):
    return jax.shard_map(
        body,
        mesh=mesh,
        in_specs=(
            P("mem", None), P(None, None, "tile", None), P(), P(), P(), P(None, "tile", None), P(None, "tile", None),
            P(), P(), P(), P(),
        ),
        out_specs=(P(None, None, "tile", "mem"), P(), P("mem", None)),
        check_vma=False,
    )
```

```python
import math

import jax
import jax.numpy as jnp
from jax import lax
from jax.experimental import pallas as pl
from jax.experimental.pallas import tpu as pltpu
from jax.sharding import PartitionSpec as P

SWEEPS = 2
STORAGE = 1.0
BF = jnp.bfloat16
F32 = jnp.float32
LANES = 128
HALO = 4
WINDOW = 32
PER_WINDOW = (WINDOW - 2) // 2
MESH = pl.DeviceIdType.MESH
BIG = 60 * 2**20


def dot(a, b):
    return jnp.dot(a, b, preferred_element_type=F32)


def dot_nt(a, b, precision=None):
    return lax.dot_general(a, b, (((1,), (1,)), ((), ())), preferred_element_type=F32, precision=precision)


def iota(shape, axis):
    return lax.broadcasted_iota(jnp.int32, shape, axis)


def ones_where(cond):
    return jnp.where(cond, 1.0, 0.0)


class Places:
    def __init__(self, side):
        self.mem, self.tile = lax.axis_index("mem"), lax.axis_index("tile")
        self.mems, self.tiles = lax.axis_size("mem"), lax.axis_size("tile")
        self.side = side
        self.plane = side * side
        self.halves = self.tiles // self.plane
        self.groups = self.mems * self.halves
        self.mine = self.mem * self.halves + self.tile // self.plane
        self.spot = lax.rem(self.tile, self.plane)

    def in_group(self, g):
        return {"mem": g // self.halves, "tile": lax.rem(g, self.halves) * self.plane + self.spot}

    def in_plane(self, at):
        return {"mem": self.mem, "tile": self.tile // self.plane * self.plane + at}


def remote(source, target, sems, index, place):
    return pltpu.make_async_remote_copy(
        src_ref=source,
        dst_ref=target,
        send_sem=sems.at[0, index],
        recv_sem=sems.at[1, index],
        device_id=place,
        device_id_type=MESH,
    )


def exchange(place, at, size, source, target, sems):
    copies = []
    for step in range(1, size):
        to = lax.rem(at + step, size)
        copies.append(remote(source(to), target.at[at], sems, step, place(to)))
        copies[-1].start()
    return copies


class RowCopies:
    def __init__(self, places, source, target, sems):
        tile, last = places.tile, places.tiles - 1
        self.has = (tile > 0, tile < last)
        to = (jnp.maximum(tile - 1, 0), jnp.minimum(tile + 1, last))
        self.copies = [
            remote(source(side), target(1 - side), sems, side, {"mem": places.mem, "tile": to[side]})
            for side in range(2)
        ]

    def start(self):
        for side in range(2):
            pl.when(self.has[side])(self.copies[side].start)

    def wait(self):
        for side in range(2):
            pl.when(self.has[side])(self.copies[side].wait_send)
            pl.when(self.has[1 - side])(self.copies[side].wait_recv)


def own_fields(every, slab, left, own_ref, mem, mems):
    members, latent = every.shape
    rows = own_ref.shape[0]
    layers = slab.shape[2]
    every = every.astype(BF).astype(F32)
    groups = latent // rows
    wide = rows * rows
    group_of = iota((1, latent), 1) // rows
    picked = jnp.concatenate([every * ones_where(group_of == g) for g in range(groups)], axis=0).astype(BF)
    spread = ones_where(lax.rem(iota((latent, wide), 0), rows) == iota((latent, wide), 1) // rows).astype(BF)
    repeated = dot(picked, spread)
    lane_row = lax.rem(iota((1, wide), 1), rows)
    for g in range(groups):
        part = repeated[g * members : (g + 1) * members]
        stacked = jnp.concatenate([part * ones_where(lane_row == r) for r in range(rows)], axis=0)
        left[:, g * wide : (g + 1) * wide] = stacked.astype(BF)
    lane = iota((1, LANES), 1)
    keep_left = (ones_where(lane >= LANES // 2) * jnp.where(mem > 0, 1.0, 0.0)).astype(BF)
    keep_right = (ones_where(lane < LANES // 2) * jnp.where(mem < mems - 1, 1.0, 0.0)).astype(BF)
    for z in range(layers):
        own = slab[0, :, z].reshape(latent * rows, LANES)
        lhs = slab[1, :, z].reshape(latent * rows, LANES)
        rhs = slab[2, :, z].reshape(latent * rows, LANES)
        both = jnp.concatenate([own, lhs * keep_left + rhs * keep_right], axis=1)
        field = dot(left[...], both).reshape(rows, members, 2 * LANES)
        own_ref[:, z * members : (z + 1) * members] = field


def decoder_weights(conv_in_ref, conv_mid_ref, conv_out_ref, taps, lift_w, mix_w, out_w, mem, mems, last):
    channels = conv_out_ref.shape[1]
    block = 4 * channels
    taps[...] = jnp.zeros_like(taps)
    taps[0:9] = conv_in_ref[...].astype(F32)
    repeat = ones_where(iota((channels, block), 0) == lax.rem(iota((channels, block), 1), channels)).astype(BF)
    in_rows = dot(taps[...].astype(BF), repeat)
    in_rows = jnp.concatenate([in_rows] * 4, axis=0)
    in_rows = (in_rows * ones_where(iota((64, block), 0) // 16 == iota((64, block), 1) // channels)).astype(BF)
    row = iota((block, 64), 0)
    col = iota((block, 64), 1)
    column = lax.rem(row, WINDOW)
    patch_row = lax.rem(row // WINDOW, 4)
    tap = lax.rem(col, 16)
    tap_row = jnp.where(tap >= 3, 1, 0) + jnp.where(tap >= 6, 1, 0)
    tap_col = tap - 3 * tap_row
    fits = (patch_row == col // 32 + tap_row) & (tap < 9)
    offset = jnp.where(fits, column - lax.rem(col // 16, 2) - tap_col, -1)
    col_of = lax.rem(iota((1, block), 1) // channels, 2)
    low, high = jnp.where(mem > 0, 1.0, 0.0), jnp.where(mem < mems - 1, 1.0, 0.0)
    for t in range(PER_WINDOW):
        weight = dot(ones_where(offset == 2 * t).astype(BF), in_rows)
        lift_w[t] = weight.astype(BF)
        if t == 0:
            lift_w[PER_WINDOW] = (weight * low).astype(BF)
        if t == 1:
            lift_w[PER_WINDOW + 1] = (weight * jnp.where(col_of == 0, low, 1.0)).astype(BF)
        if t == (last - 1) % PER_WINDOW:
            lift_w[PER_WINDOW + 2] = (weight * jnp.where(col_of == 1, high, 1.0)).astype(BF)
        if t == last % PER_WINDOW:
            lift_w[PER_WINDOW + 3] = (weight * high).astype(BF)
    mix_w[...] = jnp.zeros_like(mix_w)
    nothing = jnp.zeros((channels, channels), F32)
    for p in range(4):
        for q in range(4):
            at = ((q // 2) * 2 + p // 2) * block + ((p % 2) * 2 + q % 2) * channels
            for a in range(2):
                if not 0 <= p - a <= 2:
                    continue
                pair = [
                    conv_mid_ref[3 * (p - a) + q - b].astype(F32) if 0 <= q - b <= 2 else nothing for b in range(2)
                ]
                mix_w[at : at + channels, a * 2 * channels : (a + 1) * 2 * channels] = (
                    jnp.concatenate(pair, axis=0).T.astype(BF)
                )
    out_row = conv_out_ref[...].astype(F32)
    diag = iota((channels, channels), 0) == iota((channels, channels), 1)
    out_col = jnp.sum(jnp.where(diag, out_row, 0.0), axis=1, keepdims=True)
    out_col = jnp.concatenate([out_col] * 4, axis=0)
    group = iota((block, 2 * LANES), 0) // channels
    lane = iota((block, 2 * LANES), 1)
    match = (group // 2 == lane // LANES) & (lax.rem(group, 2) == lax.rem(lane, 2))
    out_w[...] = jnp.where(match, out_col, 0.0).astype(BF)


def pair_pieces(pieces, q, even, odd):
    lane = iota((1, LANES), 1)
    count = pieces.shape[1]

    def row_pieces(field, odd):
        own, halo = field[:, :LANES], field[:, LANES:]
        low = jnp.where(lane < LANES // 2, own, halo)
        high = jnp.where(lane < LANES // 2, halo, own)
        out = []
        for w in range(count):
            start = (WINDOW - 2) * w - HALO
            from_tile = low if w == 0 else high if w == count - 1 else own
            out.append(pltpu.roll(from_tile, (WINDOW * odd - start) % LANES, 1))
        return out

    evens, odds = row_pieces(even, 0), row_pieces(odd, 1)
    for w in range(count):
        pieces[q, w] = jnp.where(lane < WINDOW, evens[w], odds[w])


def own_windows(own_ref, pieces):
    def own_pair(q, carry):
        pair_pieces(pieces, q + HALO // 2, own_ref[2 * q], own_ref[2 * q + 1])
        return carry

    lax.fori_loop(0, own_ref.shape[0] // 2, own_pair, 0)


def all_windows(halo_ref, pieces, windows, rows):
    for half in range(HALO // 2):
        pair_pieces(pieces, half, halo_ref[2 * half].astype(F32), halo_ref[2 * half + 1].astype(F32))
        at = HALO + 2 * half
        pair_pieces(pieces, (rows + at) // 2, halo_ref[at].astype(F32), halo_ref[at + 1].astype(F32))
    lane = iota((1, LANES), 1)

    def block_row(i, carry):
        for w in range(windows.shape[0]):
            both = jnp.where(lane < LANES // 2, pieces[i, w], pltpu.roll(pieces[i + 1, w], LANES // 2, 1))
            high = both.astype(BF)
            windows[w, i] = jnp.concatenate([high, (both - high.astype(F32)).astype(BF)], axis=1)
        return carry

    lax.fori_loop(0, windows.shape[1], block_row, 0)


def convolve(windows, lift_w, mix_w, out_w, lifted, mixed, total, ends, tile, tiles, blocks):
    count, block_rows, deep, _ = windows.shape
    size = (block_rows - 1) * deep
    lane = iota((1, 2 * LANES), 1)
    pair = lax.rem(lane, LANES) // 2
    part = lane // LANES
    top = jnp.where(tile > 0, 1.0, 0.0)
    bottom = jnp.where(tile < tiles - 1, 1.0, 0.0)
    masks = {
        0: jnp.zeros((1, 2 * LANES), F32) + top,
        1: jnp.where(part == 0, top, 1.0),
        block_rows - 2: jnp.where(part == 1, bottom, 1.0),
        block_rows - 1: jnp.zeros((1, 2 * LANES), F32) + bottom,
    }

    def lift(k, slot):
        for u in range(2):
            at = jnp.minimum(2 * k + u, blocks)
            w = at // PER_WINDOW
            index = at - w * PER_WINDOW
            for special, j in enumerate((0, 1, blocks - 1, blocks)):
                index = jnp.where(at == j, PER_WINDOW + special, index)
            value = jnp.maximum(dot(windows[w].reshape(block_rows * deep, -1), lift_w[index]), 0.0)
            parts = [value[i * deep : (i + 1) * deep] for i in range(block_rows)]
            parts = [p * masks[i] if i in masks else p for i, p in enumerate(parts)]
            lifted[slot][u] = jnp.concatenate(parts, axis=0).astype(BF)

    def mix(k, slot, to):
        held = [lifted[slot].at[0], lifted[slot].at[1], lifted[(slot + 1) % 3].at[0]]
        for u in range(2):
            x, y = held[u], held[u + 1]
            lhs = jnp.concatenate([x[0:size], x[deep : deep + size], y[0:size], y[deep : deep + size]], axis=1)
            mixed[to][u] = jnp.maximum(dot(lhs, mix_w[...]), 0.0).astype(BF)

    def contract(k, at, first=False, last=False):
        even = dot(mixed[at][0], out_w[...])
        odd = dot(mixed[at][1], out_w[...])
        j = 2 * k
        if first:
            ends[...] = even
            total[...] = odd
        elif last:
            total[...] = jnp.where(pair == j - 1, even, total[...])
            ends[...] = jnp.where(pair == 0, odd, ends[...])
        else:
            total[...] = jnp.where(pair == j - 1, even, jnp.where(pair == j, odd, total[...]))

    steps = blocks // 2
    lift(0, 0)
    lift(1, 1)
    mix(0, 0, 0)
    lift(2, 2)
    contract(0, 0, first=True)
    mix(1, 1, 1)
    lift(3, 0)

    def body(q, carry):
        for v in range(6):
            k = 2 + q * 6 + v
            contract(k - 1, (1 + v) % 2)
            mix(k, (2 + v) % 3, v % 2)
            lift(k + 2, (4 + v) % 3)
        return carry

    lax.fori_loop(0, (steps - 3) // 6, body, 0)
    k = steps - 1
    contract(k - 1, (k - 1) % 2)
    mix(k, k % 3, k % 2)
    contract(k, k % 2, last=True)


def sweeps(
    own_ref, halo_ref, edge_ref, prev_ref, source_ref, total, ends, perm, first, press_ref, values,
    mem, mems, tile, tiles,
):
    rows = own_ref.shape[0]
    deep = own_ref.shape[1]
    layers = prev_ref.shape[0]
    members = deep // layers
    lane = iota((1, LANES), 1)
    top = jnp.where(tile > 0, 1.0, 0.0)
    bottom = jnp.where(tile < tiles - 1, 1.0, 0.0)
    beyond = jnp.where(lane < LANES // 2, jnp.where(mem < mems - 1, 1.0, 0.0), jnp.where(mem > 0, 1.0, 0.0))
    mine = pl.multiple_of(mem * LANES, LANES)
    before = pl.multiple_of(jnp.maximum(mem - 1, 0) * LANES, LANES)
    after = pl.multiple_of(jnp.minimum(mem + 1, mems - 1) * LANES, LANES)

    def columns(line):
        beside = jnp.where(lane < LANES // 2, line(after), line(before))
        return line(mine), beside

    def levels(pick):
        each = [columns(lambda at: pick(z, at)) for z in range(layers)]
        return [
            jnp.concatenate([jnp.broadcast_to(each[z][t], (members, LANES)) for z in range(layers)], axis=0)
            for t in range(2)
        ]

    def prev_line(index):
        r = index - 2
        if r < 0:
            return levels(lambda z, at: edge_ref[0, 2 * z + 2 + r : 2 * z + 3 + r, pl.ds(at, LANES)])
        if r >= rows:
            return levels(lambda z, at: edge_ref[1, 2 * z + r - rows : 2 * z + r - rows + 1, pl.ds(at, LANES)])
        return levels(lambda z, at: prev_ref[z, r : r + 1, pl.ds(at, LANES)])

    def source_line(index):
        r = index - 2
        if r < 0:
            return levels(lambda z, at: edge_ref[0, 4 + z : 5 + z, pl.ds(at, LANES)])
        if r >= rows:
            return levels(lambda z, at: edge_ref[1, 4 + z : 5 + z, pl.ds(at, LANES)])
        return levels(lambda z, at: source_ref[z, r : r + 1, pl.ds(at, LANES)])

    for index in range(rows + 4):
        r = index - 2
        i, a = index // 2, index % 2
        for t, parts in enumerate((total, ends)):
            value = parts[i * deep : (i + 1) * deep, a * LANES : (a + 1) * LANES]
            if 0 <= r < rows:
                field = own_ref[r, :, t * LANES : (t + 1) * LANES]
            else:
                at = HALO + r if r < 0 else HALO + r - rows
                field = halo_ref[at, :, t * LANES : (t + 1) * LANES].astype(F32)
            value = jnp.exp(field + value)
            if r < 0:
                value = jnp.where(top > 0, value, 0.0)
            if r >= rows:
                value = jnp.where(bottom > 0, value, 0.0)
            if t == 1:
                value = jnp.where(beyond > 0, value, 0.0)
            perm[index, t] = value

    def shift(own, beside, by):
        edge = LANES - 1 if by > 0 else 0
        a, b = pltpu.roll(own, -by % LANES, 1), pltpu.roll(beside, -by % LANES, 1)
        return jnp.where(lane == edge, b, a), jnp.where(lane == edge, a, b)

    def harmonic(a, b):
        both = a + b
        return jnp.where(both > 0, 2.0 * a * b / jnp.where(both > 0, both, 1.0), 0.0)

    def swap(x):
        return jnp.concatenate([x[members:], x[:members]], axis=0)

    def coefficients(index):
        here = [perm[index, t] for t in range(2)]
        right = shift(here[0], here[1], 1)
        across = [harmonic(here[t], right[t]) for t in range(2)]
        back = shift(across[0], across[1], -1)
        out = []
        for t in range(2):
            level = harmonic(here[t][:members], here[t][members:])
            out.append((across[t], back[t], jnp.concatenate([level, level], axis=0)))
        return out

    up = [harmonic(perm[0, t], perm[1, t]) for t in range(2)]
    for index in range(1, rows + 3):
        over, here, under = prev_line(index - 1), prev_line(index), prev_line(index + 1)
        down = [harmonic(perm[index, t], perm[index + 1, t]) for t in range(2)]
        coef = coefficients(index)
        right, back = shift(here[0], here[1], 1), shift(here[0], here[1], -1)
        source = source_line(index)
        for t in range(2):
            east, west, level = coef[t]
            acc = STORAGE * here[t] + source[t]
            acc = acc + down[t] * under[t] + up[t] * over[t]
            acc = acc + east * right[t] + west * back[t] + level * swap(here[t])
            first[index, t] = acc / (STORAGE + down[t] + up[t] + east + west + level)
        up = down
    up = harmonic(perm[1, 0], perm[2, 0])
    for index in range(2, rows + 2):
        r = index - 2
        down = harmonic(perm[index, 0], perm[index + 1, 0])
        east, west, level = coefficients(index)[0]
        here = first[index, 0]
        right = shift(here, first[index, 1], 1)[0]
        back = shift(here, first[index, 1], -1)[0]
        acc = STORAGE * prev_line(index)[0] + source_line(index)[0]
        acc = acc + down * first[index + 1, 0] + up * first[index - 1, 0]
        acc = acc + east * right + west * back + level * swap(here)
        press = acc / (STORAGE + down + up + east + west + level)
        up = down
        k = perm[index, 0]
        press_ref[r] = press
        for z in range(layers):
            level_press = press[z * members : (z + 1) * members]
            level_perm = k[z * members : (z + 1) * members]
            at = (z * rows + r) * LANES
            for q, value in enumerate((level_perm, level_perm * level_press)):
                high = value.astype(BF).astype(F32)
                both = jnp.concatenate([high, value - high], axis=0).astype(BF)
                values[2 * q * members : 2 * (q + 1) * members, at : at + LANES] = both


class Wells:
    def __init__(self, cells_ref, count_ref, columns, picks, places, grid_cols, grid_cells, rows):
        slots, wells = cells_ref.shape
        each = wells // places.groups
        half = LANES // 2
        ids = cells_ref[...]
        ids = jnp.where(iota((slots, wells), 0) < count_ref[...], ids, -1)
        layer = ids // grid_cells
        rest = ids - layer * grid_cells
        row = rest // grid_cols
        col = rest - row * grid_cols - places.mem * LANES
        row = row - places.tile * rows
        inside = (ids >= 0) & (row >= 0) & (row < rows) & (col >= 0) & (col < LANES)
        code = jnp.where(inside, (layer * rows + row) * LANES + col, -1)
        lane = iota((1, LANES), 1)
        tiles = []
        for t in range(places.groups // 2):
            tile = jnp.full((slots, LANES), -1, jnp.int32)
            for g in (2 * t, 2 * t + 1):
                to = half * (g % 2)
                for source in range(wells // LANES):
                    by = to - (each * g - LANES * source)
                    low, high = max(to, by), min(to + each, by + LANES)
                    if low < high:
                        moved = pltpu.roll(code[:, source * LANES : (source + 1) * LANES], by % LANES, 1)
                        tile = jnp.where((lane >= low) & (lane < high), moved, tile)
            tiles.append(tile)
        code = jnp.concatenate(tiles, axis=1)
        self.line = jnp.where(code >= 0, code // LANES, -1)
        column = jnp.where(code >= 0, lax.rem(code, LANES), -1)
        for slot in range(slots):
            columns[slot] = ones_where(iota((LANES, 1), 0) == column[slot : slot + 1]).astype(BF)
        self.columns, self.picks = columns, picks

    def fill(self, begin, end):
        slots = self.columns.shape[0]

        def each(line, carry):
            here = ones_where(self.line == line).astype(BF)
            value = self.columns[0] * here[0:1]
            for slot in range(1, slots):
                value = value + self.columns[slot] * here[slot : slot + 1]
            self.picks[pl.ds(pl.multiple_of(line * LANES, LANES), LANES)] = value
            return carry

        lax.fori_loop(begin, end, each, 0)


def main_kernel(
    lat_ref, basis_ref, prev_ref, source_ref, conv_in_ref, conv_mid_ref, conv_out_ref, cells_ref, count_ref,
    press_ref, every_ref, data_ref,
    gathered, slab, left, own, halo, send, edge, edge_send,
    taps, lift_w, mix_w, out_w, pieces, windows, l0, l1, l2, m0, m1, total, ends, perm, first, values,
    columns, picks, sums, group_in, plane_in, hold,
    slab_sems, lat_sems, edge_sems, halo_sems, group_sems, plane_sems, data_sems,
):
    side = math.isqrt(plane_in.shape[0])
    places = Places(side)
    mem, mems, tile, tiles = places.mem, places.mems, places.tile, places.tiles
    share = lat_ref.shape[0]
    members = share * mems
    layers, rows, grid_cols = prev_ref.shape
    blocks = LANES // 2 + 2

    loads = []
    for part, offset in enumerate((0, -1, 1)):
        at = jnp.clip(mem + offset, 0, mems - 1)
        loads.append(
            pltpu.make_async_copy(
                basis_ref.at[:, :, :, pl.ds(pl.multiple_of(at * LANES, LANES), LANES)],
                slab.at[part],
                slab_sems.at[part],
            )
        )
    for load in loads:
        load.start()

    barrier = pltpu.get_barrier_semaphore()
    for step in range(1, places.groups):
        to = places.in_group(lax.rem(places.mine + step, places.groups))
        pl.semaphore_signal(barrier, inc=1, device_id=to, device_id_type=MESH)
    for step in range(1, places.plane):
        to = places.in_plane(lax.rem(places.spot + step, places.plane))
        pl.semaphore_signal(barrier, inc=1, device_id=to, device_id_type=MESH)
    for ends_at, to in ((places.plane - 1, tile + 1), (0, tile - 1)):

        @pl.when((places.spot == ends_at) & (to >= 0) & (to < tiles))
        def _(to=to):
            pl.semaphore_signal(barrier, inc=1, device_id={"mem": mem, "tile": to}, device_id_type=MESH)

    decoder_weights(conv_in_ref, conv_mid_ref, conv_out_ref, taps, lift_w, mix_w, out_w, mem, mems, blocks)
    for side_at in range(2):
        begin = 0 if side_at == 0 else rows - 2
        at = 0 if side_at == 0 else rows - 1
        for z in range(layers):
            edge_send[side_at, 2 * z : 2 * z + 2] = prev_ref[z, begin : begin + 2]
            edge_send[side_at, 4 + z : 5 + z] = source_ref[z, at : at + 1]
        edge_send[side_at, 6:8] = jnp.zeros((2, grid_cols), F32)
    for side_at, at_end in ((0, tile == 0), (1, tile == tiles - 1)):

        @pl.when(at_end)
        def _(side_at=side_at):
            edge[side_at] = jnp.zeros(edge.shape[1:], F32)
            halo[side_at * HALO : (side_at + 1) * HALO] = jnp.zeros((HALO, *halo.shape[1:]), BF)

    at_last = places.spot // (places.plane - 1) * jnp.minimum(tiles - 1 - tile, 1)
    at_first = (places.plane - 1 - places.spot) // (places.plane - 1) * jnp.minimum(tile, 1)
    pl.semaphore_wait(barrier, places.groups + places.plane - 2 + at_last + at_first)

    def in_mem(at):
        return {"mem": at, "tile": tile}

    lat_copies = exchange(in_mem, mem, mems, lambda to: lat_ref, gathered, lat_sems)
    edge_copies = RowCopies(places, lambda s: edge_send.at[s], lambda s: edge.at[s], edge_sems)
    edge_copies.start()
    wells = Wells(cells_ref, count_ref, columns, picks, places, grid_cols, grid_cols * rows * tiles, rows)
    lines = layers * rows
    wells.fill(0, lines // 2)
    gathered[mem] = lat_ref[...]
    for copy in lat_copies:
        copy.wait()
    for s in range(mems):
        every_ref[share * s : share * (s + 1)] = gathered[s]
    for load in loads:
        load.wait()
    own_fields(every_ref[...], slab, left, own, mem, mems)
    send[0:HALO] = own[0:HALO].astype(BF)
    send[HALO : 2 * HALO] = own[rows - HALO : rows].astype(BF)
    halo_copies = RowCopies(
        places,
        lambda s: send.at[pl.ds(s * HALO, HALO)],
        lambda s: halo.at[pl.ds(s * HALO, HALO)],
        halo_sems,
    )
    halo_copies.start()
    own_windows(own, pieces)
    wells.fill(lines // 2, lines)
    edge_copies.wait()
    halo_copies.wait()
    all_windows(halo, pieces, windows, rows)
    convolve(windows, lift_w, mix_w, out_w, (l0, l1, l2), (m0, m1), total, ends, tile, tiles, blocks)
    sweeps(
        own, halo, edge, prev_ref, source_ref, total, ends, perm, first, press_ref, values, mem, mems, tile, tiles
    )

    got = dot(values[...], picks[...])
    weight = got[0:members] + got[members : 2 * members]
    number = got[2 * members : 3 * members] + got[3 * members : 4 * members]
    low = iota((1, LANES), 1) < LANES // 2
    for t in range(places.groups // 2):
        n, w = number[:, t * LANES : (t + 1) * LANES], weight[:, t * LANES : (t + 1) * LANES]
        sums[2 * t] = jnp.where(low, n, pltpu.roll(w, LANES // 2, 1))
        sums[2 * t + 1] = jnp.where(low, pltpu.roll(n, LANES // 2, 1), w)

    def together(target):
        value = target[0]
        for at in range(1, target.shape[0]):
            value = value + target[at]
        return value

    group_copies = exchange(places.in_group, places.mine, places.groups, lambda to: sums.at[to], group_in, group_sems)
    group_in[places.mine] = sums[places.mine]
    for copy in group_copies:
        copy.wait()
    value = together(group_in)
    hold[0] = value
    plane_in[places.spot] = value
    plane_copies = exchange(places.in_plane, places.spot, places.plane, lambda to: hold.at[0], plane_in, plane_sems)
    for copy in plane_copies:
        copy.wait()
    value = together(plane_in)
    value = value / pltpu.roll(value, LANES // 2, 1)
    hold[1] = value
    data_ref[places.mine] = value
    data_copies = exchange(places.in_group, places.mine, places.groups, lambda to: hold.at[1], data_ref, data_sems)
    for copy in data_copies:
        copy.wait()


def main(latents, basis, prev, source, conv_in, conv_mid, conv_out, perf_cells, perf_count):
    share, latent = latents.shape
    mems, tiles = lax.axis_size("mem"), lax.axis_size("tile")
    members = share * mems
    _, layers, rows, width = basis.shape
    deep = layers * members
    channels = conv_in.shape[1]
    block = 4 * channels
    blocks = LANES // 2 + 2
    count = blocks // PER_WINDOW + 1
    out_rows = rows // 2 + 2
    slots = perf_cells.shape[1]
    plane = tiles // 2
    groups = 2 * mems
    lanes = groups // 2 * LANES
    vmem = pl.BlockSpec(memory_space=pltpu.VMEM)
    piece = (members, LANES)
    return pl.pallas_call(
        main_kernel,
        out_shape=[
            jax.ShapeDtypeStruct((rows, deep, LANES), F32),
            jax.ShapeDtypeStruct((members, latent), F32),
            jax.ShapeDtypeStruct((groups, *piece), F32),
        ],
        in_specs=[vmem, pl.BlockSpec(memory_space=pl.ANY)] + [vmem] * 7,
        out_specs=[vmem] * 3,
        scratch_shapes=[
            pltpu.VMEM((mems, share, latent), F32),
            pltpu.VMEM((3, latent, layers, rows, LANES), BF),
            pltpu.VMEM((rows * members, latent * rows), BF),
            pltpu.VMEM((rows, deep, 2 * LANES), F32),
            pltpu.VMEM((2 * HALO, deep, 2 * LANES), BF),
            pltpu.VMEM((2 * HALO, deep, 2 * LANES), BF),
            pltpu.VMEM((2, 8, width), F32),
            pltpu.VMEM((2, 8, width), F32),
            pltpu.VMEM((16, channels), F32),
            pltpu.VMEM((PER_WINDOW + 4, block, block), BF),
            pltpu.VMEM((4 * block, block), BF),
            pltpu.VMEM((block, 2 * LANES), BF),
            pltpu.VMEM((rows // 2 + HALO, count, deep, LANES), F32),
            pltpu.VMEM((count, out_rows + 1, deep, 2 * LANES), BF),
        ]
        + [pltpu.VMEM((2, (out_rows + 1) * deep, block), BF)] * 3
        + [pltpu.VMEM((2, out_rows * deep, block), BF)] * 2
        + [pltpu.VMEM((out_rows * deep, 2 * LANES), F32)] * 2
        + [pltpu.VMEM((rows + 4, 2, deep, LANES), F32)] * 2
        + [
            pltpu.VMEM((4 * members, layers * rows * LANES), BF),
            pltpu.VMEM((slots, LANES, lanes), BF),
            pltpu.VMEM((layers * rows * LANES, lanes), BF),
            pltpu.VMEM((groups, *piece), F32),
            pltpu.VMEM((groups, *piece), F32),
            pltpu.VMEM((plane, *piece), F32),
            pltpu.VMEM((2, *piece), F32),
            pltpu.SemaphoreType.DMA((3,)),
            pltpu.SemaphoreType.DMA((2, mems)),
            pltpu.SemaphoreType.DMA((2, 2)),
            pltpu.SemaphoreType.DMA((2, 2)),
            pltpu.SemaphoreType.DMA((2, groups)),
            pltpu.SemaphoreType.DMA((2, plane)),
            pltpu.SemaphoreType.DMA((2, groups)),
        ],
        compiler_params=pltpu.CompilerParams(collective_id=0, has_side_effects=True, vmem_limit_bytes=BIG),
        name="main",
    )(latents, basis, prev, source, conv_in, conv_mid, conv_out.reshape(1, channels), perf_cells.T,
      perf_count.reshape(1, -1))


def update_kernel(raw_ref, data_ref, every_ref, obs_ref, error_ref, press_ref, well_ref, new_ref):
    mem, mems = lax.axis_index("mem"), lax.axis_size("mem")
    groups, members, _ = data_ref.shape
    layers = press_ref.shape[1]
    for r in range(press_ref.shape[2]):
        for z in range(layers):
            press_ref[:, z, r, :] = raw_ref[r, z * members : (z + 1) * members]
    each = obs_ref.shape[1] // groups
    lane = iota((1, LANES), 1)
    parts = []
    for t in range(obs_ref.shape[1] // LANES):
        part = jnp.zeros((members, LANES), F32)
        for g in range(groups):
            by = each * g - LANES * t
            if by <= -each or by >= LANES:
                continue
            moved = pltpu.roll(data_ref[g], by % LANES, 1)
            part = jnp.where((lane >= by) & (lane < by + each), moved, part)
        parts.append(part)
    wells = jnp.concatenate(parts, axis=1)
    well_ref[...] = wells
    scale = 2.0 * error_ref[...]
    centred = wells - jnp.sum(wells, axis=0, keepdims=True) / members
    scaled = centred / (math.sqrt(members - 1) * scale)
    innov = (obs_ref[...] - wells) / scale
    exact = lax.Precision.HIGHEST
    eye = ones_where(iota((members, members), 0) == iota((members, members), 1))
    gram = eye + dot_nt(scaled, scaled, exact)
    cross = dot_nt(innov, scaled, exact)
    work = jnp.concatenate([gram, eye], axis=1)
    row_at = iota((members, 1), 0)
    for k in range(members):
        line = work[k : k + 1] / work[k : k + 1, k : k + 1]
        work = jnp.where(row_at == k, line, work - work[:, k : k + 1] * line)
    inverse = work[:, members:]
    weights = jnp.dot(cross, inverse, preferred_element_type=F32, precision=exact)
    every = every_ref[...]
    spread = (every - jnp.sum(every, axis=0, keepdims=True) / members) / math.sqrt(members - 1)
    new = every + jnp.dot(weights, spread, preferred_element_type=F32, precision=exact)
    share = members // mems
    own = new[0:share]
    for s in range(1, mems):
        own = jnp.where(mem == s, new[s * share : (s + 1) * share], own)
    new_ref[...] = own


def update(raw, data, every, obs, error):
    rows, deep, _ = raw.shape
    _, members, _ = data.shape
    vmem = pl.BlockSpec(memory_space=pltpu.VMEM)
    return pl.pallas_call(
        update_kernel,
        out_shape=[
            jax.ShapeDtypeStruct((members, deep // members, rows, LANES), F32),
            jax.ShapeDtypeStruct(obs.shape, F32),
            jax.ShapeDtypeStruct((members // lax.axis_size("mem"), every.shape[1]), F32),
        ],
        in_specs=[vmem] * 5,
        out_specs=[vmem] * 3,
        name="update",
    )(raw, data, every, obs, error.reshape(1, -1))


def body(
    latents, basis, conv_in, conv_mid, conv_out, pressure_prev, source, perf_cells, perf_count, obs_perturbed, obs_error
):
    raw, every, data = main(
        latents, basis, pressure_prev, source, conv_in, conv_mid, conv_out, perf_cells, perf_count
    )
    return tuple(update(raw, data, every, obs_perturbed, obs_error))


def solution(mesh):
    return jax.shard_map(
        body,
        mesh=mesh,
        in_specs=(
            P("mem", None), P(None, None, "tile", None), P(), P(), P(), P(None, "tile", None), P(None, "tile", None),
            P(), P(), P(), P(),
        ),
        out_specs=(P(None, None, "tile", "mem"), P(), P("mem", None)),
        check_vma=False,
    )
```

```python
import math

import jax
import jax.numpy as jnp
from jax import lax
from jax.experimental import pallas as pl
from jax.experimental.pallas import tpu as pltpu
from jax.sharding import PartitionSpec as P

SWEEPS = 2
STORAGE = 1.0
BF = jnp.bfloat16
F32 = jnp.float32
LANES = 128
HALO = 4
WINDOW = 32
PER_WINDOW = (WINDOW - 2) // 2
MESH = pl.DeviceIdType.MESH
BIG = 60 * 2**20


def dot(a, b):
    return jnp.dot(a, b, preferred_element_type=F32)


def dot_nt(a, b, precision=None):
    return lax.dot_general(a, b, (((1,), (1,)), ((), ())), preferred_element_type=F32, precision=precision)


def iota(shape, axis):
    return lax.broadcasted_iota(jnp.int32, shape, axis)


def ones_where(cond):
    return jnp.where(cond, 1.0, 0.0)


class Places:
    def __init__(self, side):
        self.mem, self.tile = lax.axis_index("mem"), lax.axis_index("tile")
        self.mems, self.tiles = lax.axis_size("mem"), lax.axis_size("tile")
        self.side = side
        self.plane = side * side
        self.halves = self.tiles // self.plane
        self.groups = self.mems * self.halves
        self.mine = self.mem * self.halves + self.tile // self.plane
        self.spot = lax.rem(self.tile, self.plane)

    def in_group(self, g):
        return {"mem": g // self.halves, "tile": lax.rem(g, self.halves) * self.plane + self.spot}

    def in_plane(self, at):
        return {"mem": self.mem, "tile": self.tile // self.plane * self.plane + at}


def remote(source, target, sems, index, place):
    return pltpu.make_async_remote_copy(
        src_ref=source,
        dst_ref=target,
        send_sem=sems.at[0, index],
        recv_sem=sems.at[1, index],
        device_id=place,
        device_id_type=MESH,
    )


def exchange(place, at, size, source, target, sems):
    copies = []
    for step in range(1, size):
        to = lax.rem(at + step, size)
        copies.append(remote(source(to), target.at[at], sems, step, place(to)))
        copies[-1].start()
    return copies


class RowCopies:
    def __init__(self, places, source, target, sems):
        tile, last = places.tile, places.tiles - 1
        self.has = (tile > 0, tile < last)
        to = (jnp.maximum(tile - 1, 0), jnp.minimum(tile + 1, last))
        self.copies = [
            remote(source(side), target(1 - side), sems, side, {"mem": places.mem, "tile": to[side]})
            for side in range(2)
        ]

    def start(self):
        for side in range(2):
            pl.when(self.has[side])(self.copies[side].start)

    def wait(self):
        for side in range(2):
            pl.when(self.has[side])(self.copies[side].wait_send)
            pl.when(self.has[1 - side])(self.copies[side].wait_recv)


def own_fields(every, slab, left, own_ref, mem, mems):
    members, latent = every.shape
    rows = own_ref.shape[0]
    layers = slab.shape[2]
    every = every.astype(BF).astype(F32)
    groups = latent // rows
    wide = rows * rows
    group_of = iota((1, latent), 1) // rows
    picked = jnp.concatenate([every * ones_where(group_of == g) for g in range(groups)], axis=0).astype(BF)
    spread = ones_where(lax.rem(iota((latent, wide), 0), rows) == iota((latent, wide), 1) // rows).astype(BF)
    repeated = dot(picked, spread)
    lane_row = lax.rem(iota((1, wide), 1), rows)
    for g in range(groups):
        part = repeated[g * members : (g + 1) * members]
        stacked = jnp.concatenate([part * ones_where(lane_row == r) for r in range(rows)], axis=0)
        left[:, g * wide : (g + 1) * wide] = stacked.astype(BF)
    lane = iota((1, LANES), 1)
    keep_left = (ones_where(lane >= LANES // 2) * jnp.where(mem > 0, 1.0, 0.0)).astype(BF)
    keep_right = (ones_where(lane < LANES // 2) * jnp.where(mem < mems - 1, 1.0, 0.0)).astype(BF)
    for z in range(layers):
        own = slab[0, :, z].reshape(latent * rows, LANES)
        lhs = slab[1, :, z].reshape(latent * rows, LANES)
        rhs = slab[2, :, z].reshape(latent * rows, LANES)
        both = jnp.concatenate([own, lhs * keep_left + rhs * keep_right], axis=1)
        field = dot(left[...], both).reshape(rows, members, 2 * LANES)
        own_ref[:, z * members : (z + 1) * members] = field


def decoder_weights(conv_in_ref, conv_mid_ref, conv_out_ref, taps, lift_w, mix_w, out_w, scale, mem, mems, last):
    channels = conv_out_ref.shape[1]
    block = 4 * channels
    taps[...] = jnp.zeros_like(taps)
    taps[0:9] = conv_in_ref[...].astype(F32)
    repeat = ones_where(iota((channels, block), 0) == lax.rem(iota((channels, block), 1), channels)).astype(BF)
    in_rows = dot(taps[...].astype(BF), repeat)
    in_rows = jnp.concatenate([in_rows] * 4, axis=0)
    in_rows = (in_rows * ones_where(iota((64, block), 0) // 16 == iota((64, block), 1) // channels)).astype(BF)
    row = iota((block, 64), 0)
    col = iota((block, 64), 1)
    column = lax.rem(row, WINDOW)
    patch_row = lax.rem(row // WINDOW, 4)
    tap = lax.rem(col, 16)
    tap_row = jnp.where(tap >= 3, 1, 0) + jnp.where(tap >= 6, 1, 0)
    tap_col = tap - 3 * tap_row
    fits = (patch_row == col // 32 + tap_row) & (tap < 9)
    offset = jnp.where(fits, column - lax.rem(col // 16, 2) - tap_col, -1)
    col_of = lax.rem(iota((1, block), 1) // channels, 2)
    low, high = jnp.where(mem > 0, 1.0, 0.0), jnp.where(mem < mems - 1, 1.0, 0.0)
    for t in range(PER_WINDOW):
        weight = dot(ones_where(offset == 2 * t).astype(BF), in_rows)
        lift_w[t] = weight.astype(BF)
        if t == 0:
            lift_w[PER_WINDOW] = (weight * low).astype(BF)
        if t == 1:
            lift_w[PER_WINDOW + 1] = (weight * jnp.where(col_of == 0, low, 1.0)).astype(BF)
        if t == (last - 1) % PER_WINDOW:
            lift_w[PER_WINDOW + 2] = (weight * jnp.where(col_of == 1, high, 1.0)).astype(BF)
        if t == last % PER_WINDOW:
            lift_w[PER_WINDOW + 3] = (weight * high).astype(BF)
    mix_w[...] = jnp.zeros_like(mix_w)
    nothing = jnp.zeros((channels, channels), F32)
    for p in range(4):
        for q in range(4):
            at = ((q // 2) * 2 + p // 2) * block + ((p % 2) * 2 + q % 2) * channels
            for a in range(2):
                if not 0 <= p - a <= 2:
                    continue
                pair = [
                    conv_mid_ref[3 * (p - a) + q - b].astype(F32) if 0 <= q - b <= 2 else nothing for b in range(2)
                ]
                mix_w[at : at + channels, a * 2 * channels : (a + 1) * 2 * channels] = (
                    jnp.concatenate(pair, axis=0).T.astype(BF)
                )
    out_row = conv_out_ref[...].astype(F32)
    scale[...] = jnp.concatenate([out_row] * 4, axis=1)
    row = iota((block, 2 * LANES), 0)
    lane = iota((block, 2 * LANES), 1)
    match = (row // LANES == lane // LANES) & (lax.rem(row // (LANES // 2), 2) == lax.rem(lane, 2))
    match = match & (lax.rem(row // (LANES // 4), 2) == lax.rem(lane // (LANES // 2), 2))
    out_w[...] = ones_where(match).astype(BF)


def pair_pieces(pieces, q, even, odd):
    lane = iota((1, LANES), 1)
    count = pieces.shape[1]

    def row_pieces(field, odd):
        own, halo = field[:, :LANES], field[:, LANES:]
        low = jnp.where(lane < LANES // 2, own, halo)
        high = jnp.where(lane < LANES // 2, halo, own)
        out = []
        for w in range(count):
            start = (WINDOW - 2) * w - HALO
            from_tile = low if w == 0 else high if w == count - 1 else own
            out.append(pltpu.roll(from_tile, (WINDOW * odd - start) % LANES, 1))
        return out

    evens, odds = row_pieces(even, 0), row_pieces(odd, 1)
    for w in range(count):
        pieces[q, w] = jnp.where(lane < WINDOW, evens[w], odds[w])


def own_windows(own_ref, pieces):
    def own_pair(q, carry):
        pair_pieces(pieces, q + HALO // 2, own_ref[2 * q], own_ref[2 * q + 1])
        return carry

    lax.fori_loop(0, own_ref.shape[0] // 2, own_pair, 0)


def all_windows(halo_ref, pieces, windows, rows):
    for half in range(HALO // 2):
        pair_pieces(pieces, half, halo_ref[2 * half].astype(F32), halo_ref[2 * half + 1].astype(F32))
        at = HALO + 2 * half
        pair_pieces(pieces, (rows + at) // 2, halo_ref[at].astype(F32), halo_ref[at + 1].astype(F32))
    lane = iota((1, LANES), 1)

    def block_row(i, carry):
        for w in range(windows.shape[0]):
            both = jnp.where(lane < LANES // 2, pieces[i, w], pltpu.roll(pieces[i + 1, w], LANES // 2, 1))
            high = both.astype(BF)
            windows[w, i] = jnp.concatenate([high, (both - high.astype(F32)).astype(BF)], axis=1)
        return carry

    lax.fori_loop(0, windows.shape[1], block_row, 0)


def convolve(windows, lift_w, mix_w, out_w, scale, lifted, mixed, total, ends, tile, tiles, blocks):
    count, block_rows, deep, _ = windows.shape
    size = (block_rows - 1) * deep
    lane = iota((1, 2 * LANES), 1)
    half = lax.rem(lane, LANES // 2)
    part = lane // LANES
    top = jnp.where(tile > 0, 1.0, 0.0)
    bottom = jnp.where(tile < tiles - 1, 1.0, 0.0)
    masks = {
        0: jnp.zeros((1, 2 * LANES), F32) + top,
        1: jnp.where(part == 0, top, 1.0),
        block_rows - 2: jnp.where(part == 1, bottom, 1.0),
        block_rows - 1: jnp.zeros((1, 2 * LANES), F32) + bottom,
    }
    steps = (blocks - 2) // 2
    streams = (lambda t: 1 + t, lambda t: 1 + steps + t)

    def lift(places, slot):
        for u in range(2):
            at = places[u]
            if isinstance(at, int) and at in (0, 1, blocks - 1, blocks):
                w, index = at // PER_WINDOW, PER_WINDOW + (0, 1, blocks - 1, blocks).index(at)
            else:
                at = jnp.minimum(at, blocks)
                w = at // PER_WINDOW
                index = at - w * PER_WINDOW
                for special, j in ((2, blocks - 1), (3, blocks)):
                    index = jnp.where(at == j, PER_WINDOW + special, index)
            value = jnp.maximum(dot(windows[w].reshape(block_rows * deep, -1), lift_w[index]), 0.0)
            parts = [value[i * deep : (i + 1) * deep] for i in range(block_rows)]
            parts = [p * masks[i] if i in masks else p for i, p in enumerate(parts)]
            lifted[slot][u] = jnp.concatenate(parts, axis=0).astype(BF)

    def mix(slot, to):
        for u in range(2):
            x, y = lifted[slot].at[u], lifted[(slot + 1) % 3].at[u]
            lhs = jnp.concatenate([x[0:size], x[deep : deep + size], y[0:size], y[deep : deep + size]], axis=1)
            value = jnp.maximum(dot(lhs, mix_w[...]), 0.0) * scale[...]
            by = LANES - LANES // 4 if u == 0 else LANES // 4
            other = [pltpu.roll(value[:, i * LANES : (i + 1) * LANES], by, 1) for i in range(2)]
            mixed[to][u] = (value + jnp.concatenate(other, axis=1)).astype(BF)

    keep = [ones_where(half < LANES // 4).astype(BF), ones_where(half >= LANES // 4).astype(BF)]

    def both_streams(at):
        return mixed[at][0] * keep[0] + mixed[at][1] * keep[1]

    def contract(t, at):
        total[...] = jnp.where(half // 2 == t, dot(both_streams(at), out_w[...]), total[...])

    def ahead(t):
        return [stream(t) for stream in streams]

    total[...] = jnp.zeros_like(total)
    lift(ahead(0), 0)
    lift(ahead(1), 1)
    mix(0, 0)
    lift(ahead(2), 2)

    def body(q, carry):
        for v in range(6):
            t = 1 + q * 6 + v
            contract(t - 1, v % 2)
            mix((1 + v) % 3, (1 + v) % 2)
            lift(ahead(t + 2), v % 3)
        return carry

    whole = (steps - 2) // 6
    lax.fori_loop(0, whole, body, 0)
    for t in range(1 + 6 * whole, steps):
        contract(t - 1, (t - 1) % 2)
        mix(t % 3, t % 2)
        if t < steps - 1:
            lift(ahead(t + 2), (t + 2) % 3)
    contract(steps - 1, (steps - 1) % 2)
    lift((0, blocks - 1), 0)
    lift((1, blocks), 1)
    mix(0, 0)
    value = dot(both_streams(0), out_w[...])
    swapped = [pltpu.roll(value[:, i * LANES : (i + 1) * LANES], LANES // 2, 1) for i in range(2)]
    ends[...] = jnp.concatenate(swapped, axis=1)


def sweeps(
    own_ref, halo_ref, edge_ref, prev_ref, source_ref, total, ends, perm, first, press_ref, values,
    mem, mems, tile, tiles,
):
    rows = own_ref.shape[0]
    deep = own_ref.shape[1]
    layers = prev_ref.shape[0]
    members = deep // layers
    lane = iota((1, LANES), 1)
    top = jnp.where(tile > 0, 1.0, 0.0)
    bottom = jnp.where(tile < tiles - 1, 1.0, 0.0)
    beyond = jnp.where(lane < LANES // 2, jnp.where(mem < mems - 1, 1.0, 0.0), jnp.where(mem > 0, 1.0, 0.0))
    mine = pl.multiple_of(mem * LANES, LANES)
    before = pl.multiple_of(jnp.maximum(mem - 1, 0) * LANES, LANES)
    after = pl.multiple_of(jnp.minimum(mem + 1, mems - 1) * LANES, LANES)

    def columns(line):
        beside = jnp.where(lane < LANES // 2, line(after), line(before))
        return line(mine), beside

    def levels(pick):
        each = [columns(lambda at: pick(z, at)) for z in range(layers)]
        return [
            jnp.concatenate([jnp.broadcast_to(each[z][t], (members, LANES)) for z in range(layers)], axis=0)
            for t in range(2)
        ]

    def prev_line(index):
        r = index - 2
        if r < 0:
            return levels(lambda z, at: edge_ref[0, 2 * z + 2 + r : 2 * z + 3 + r, pl.ds(at, LANES)])
        if r >= rows:
            return levels(lambda z, at: edge_ref[1, 2 * z + r - rows : 2 * z + r - rows + 1, pl.ds(at, LANES)])
        return levels(lambda z, at: prev_ref[z, r : r + 1, pl.ds(at, LANES)])

    def source_line(index):
        r = index - 2
        if r < 0:
            return levels(lambda z, at: edge_ref[0, 4 + z : 5 + z, pl.ds(at, LANES)])
        if r >= rows:
            return levels(lambda z, at: edge_ref[1, 4 + z : 5 + z, pl.ds(at, LANES)])
        return levels(lambda z, at: source_ref[z, r : r + 1, pl.ds(at, LANES)])

    for index in range(rows + 4):
        r = index - 2
        i, a = index // 2, index % 2
        for t, parts in enumerate((total, ends)):
            value = parts[i * deep : (i + 1) * deep, a * LANES : (a + 1) * LANES]
            if 0 <= r < rows:
                field = own_ref[r, :, t * LANES : (t + 1) * LANES]
            else:
                at = HALO + r if r < 0 else HALO + r - rows
                field = halo_ref[at, :, t * LANES : (t + 1) * LANES].astype(F32)
            value = jnp.exp(field + value)
            if r < 0:
                value = jnp.where(top > 0, value, 0.0)
            if r >= rows:
                value = jnp.where(bottom > 0, value, 0.0)
            if t == 1:
                value = jnp.where(beyond > 0, value, 0.0)
            perm[index, t] = value

    def shift(own, beside, by):
        edge = LANES - 1 if by > 0 else 0
        a, b = pltpu.roll(own, -by % LANES, 1), pltpu.roll(beside, -by % LANES, 1)
        return jnp.where(lane == edge, b, a), jnp.where(lane == edge, a, b)

    def harmonic(a, b):
        both = a + b
        return jnp.where(both > 0, 2.0 * a * b / jnp.where(both > 0, both, 1.0), 0.0)

    def swap(x):
        return jnp.concatenate([x[members:], x[:members]], axis=0)

    def coefficients(index):
        here = [perm[index, t] for t in range(2)]
        right = shift(here[0], here[1], 1)
        across = [harmonic(here[t], right[t]) for t in range(2)]
        back = shift(across[0], across[1], -1)
        out = []
        for t in range(2):
            level = harmonic(here[t][:members], here[t][members:])
            out.append((across[t], back[t], jnp.concatenate([level, level], axis=0)))
        return out

    up = [harmonic(perm[0, t], perm[1, t]) for t in range(2)]
    for index in range(1, rows + 3):
        over, here, under = prev_line(index - 1), prev_line(index), prev_line(index + 1)
        down = [harmonic(perm[index, t], perm[index + 1, t]) for t in range(2)]
        coef = coefficients(index)
        right, back = shift(here[0], here[1], 1), shift(here[0], here[1], -1)
        source = source_line(index)
        for t in range(2):
            east, west, level = coef[t]
            acc = STORAGE * here[t] + source[t]
            acc = acc + down[t] * under[t] + up[t] * over[t]
            acc = acc + east * right[t] + west * back[t] + level * swap(here[t])
            first[index, t] = acc / (STORAGE + down[t] + up[t] + east + west + level)
        up = down
    up = harmonic(perm[1, 0], perm[2, 0])
    for index in range(2, rows + 2):
        r = index - 2
        down = harmonic(perm[index, 0], perm[index + 1, 0])
        east, west, level = coefficients(index)[0]
        here = first[index, 0]
        right = shift(here, first[index, 1], 1)[0]
        back = shift(here, first[index, 1], -1)[0]
        acc = STORAGE * prev_line(index)[0] + source_line(index)[0]
        acc = acc + down * first[index + 1, 0] + up * first[index - 1, 0]
        acc = acc + east * right + west * back + level * swap(here)
        press = acc / (STORAGE + down + up + east + west + level)
        up = down
        k = perm[index, 0]
        press_ref[r] = press
        for z in range(layers):
            level_press = press[z * members : (z + 1) * members]
            level_perm = k[z * members : (z + 1) * members]
            at = (z * rows + r) * LANES
            for q, value in enumerate((level_perm, level_perm * level_press)):
                high = value.astype(BF).astype(F32)
                both = jnp.concatenate([high, value - high], axis=0).astype(BF)
                values[2 * q * members : 2 * (q + 1) * members, at : at + LANES] = both


class Wells:
    def __init__(self, cells_ref, count_ref, columns, picks, places, grid_cols, grid_cells, rows):
        slots, wells = cells_ref.shape
        each = wells // places.groups
        half = LANES // 2
        ids = cells_ref[...]
        ids = jnp.where(iota((slots, wells), 0) < count_ref[...].reshape(1, wells), ids, -1)
        layer = ids // grid_cells
        rest = ids - layer * grid_cells
        row = rest // grid_cols
        col = rest - row * grid_cols - places.mem * LANES
        row = row - places.tile * rows
        inside = (ids >= 0) & (row >= 0) & (row < rows) & (col >= 0) & (col < LANES)
        code = jnp.where(inside, (layer * rows + row) * LANES + col, -1)
        lane = iota((1, LANES), 1)
        tiles = []
        for t in range(places.groups // 2):
            tile = jnp.full((slots, LANES), -1, jnp.int32)
            for g in (2 * t, 2 * t + 1):
                to = half * (g % 2)
                for source in range(wells // LANES):
                    by = to - (each * g - LANES * source)
                    low, high = max(to, by), min(to + each, by + LANES)
                    if low < high:
                        moved = pltpu.roll(code[:, source * LANES : (source + 1) * LANES], by % LANES, 1)
                        tile = jnp.where((lane >= low) & (lane < high), moved, tile)
            tiles.append(tile)
        code = jnp.concatenate(tiles, axis=1)
        self.line = jnp.where(code >= 0, code // LANES, -1)
        column = jnp.where(code >= 0, lax.rem(code, LANES), -1)
        for slot in range(slots):
            columns[slot] = ones_where(iota((LANES, 1), 0) == column[slot : slot + 1]).astype(BF)
        self.columns, self.picks = columns, picks

    def fill(self, begin, end):
        slots = self.columns.shape[0]

        def each(line, carry):
            here = ones_where(self.line == line).astype(BF)
            value = self.columns[0] * here[0:1]
            for slot in range(1, slots):
                value = value + self.columns[slot] * here[slot : slot + 1]
            self.picks[pl.ds(pl.multiple_of(line * LANES, LANES), LANES)] = value
            return carry

        lax.fori_loop(begin, end, each, 0)


def main_kernel(
    lat_ref, basis_ref, prev_ref, source_ref, conv_in_ref, conv_mid_ref, conv_out_ref, cells_ref, count_ref,
    press_ref, every_ref, data_ref,
    raw, gathered, slab, left, own, halo, send, edge, edge_send,
    taps, lift_w, mix_w, out_w, scale, pieces, windows, l0, l1, l2, m0, m1, total, ends, perm, first, values,
    columns, picks, sums, group_in, plane_in, hold,
    slab_sems, lat_sems, edge_sems, halo_sems, group_sems, plane_sems, data_sems,
):
    side = math.isqrt(plane_in.shape[0])
    places = Places(side)
    mem, mems, tile, tiles = places.mem, places.mems, places.tile, places.tiles
    share = lat_ref.shape[0]
    members = share * mems
    layers, rows, grid_cols = prev_ref.shape
    blocks = LANES // 2 + 2

    loads = []
    for part, offset in enumerate((0, -1, 1)):
        at = jnp.clip(mem + offset, 0, mems - 1)
        loads.append(
            pltpu.make_async_copy(
                basis_ref.at[:, :, :, pl.ds(pl.multiple_of(at * LANES, LANES), LANES)],
                slab.at[part],
                slab_sems.at[part],
            )
        )
    for load in loads:
        load.start()

    barrier = pltpu.get_barrier_semaphore()
    for step in range(1, places.groups):
        to = places.in_group(lax.rem(places.mine + step, places.groups))
        pl.semaphore_signal(barrier, inc=1, device_id=to, device_id_type=MESH)
    for step in range(1, places.plane):
        to = places.in_plane(lax.rem(places.spot + step, places.plane))
        pl.semaphore_signal(barrier, inc=1, device_id=to, device_id_type=MESH)
    for ends_at, to in ((places.plane - 1, tile + 1), (0, tile - 1)):

        @pl.when((places.spot == ends_at) & (to >= 0) & (to < tiles))
        def _(to=to):
            pl.semaphore_signal(barrier, inc=1, device_id={"mem": mem, "tile": to}, device_id_type=MESH)

    decoder_weights(conv_in_ref, conv_mid_ref, conv_out_ref, taps, lift_w, mix_w, out_w, scale, mem, mems, blocks)
    for side_at in range(2):
        begin = 0 if side_at == 0 else rows - 2
        at = 0 if side_at == 0 else rows - 1
        for z in range(layers):
            edge_send[side_at, 2 * z : 2 * z + 2] = prev_ref[z, begin : begin + 2]
            edge_send[side_at, 4 + z : 5 + z] = source_ref[z, at : at + 1]
        edge_send[side_at, 6:8] = jnp.zeros((2, grid_cols), F32)
    for side_at, at_end in ((0, tile == 0), (1, tile == tiles - 1)):

        @pl.when(at_end)
        def _(side_at=side_at):
            edge[side_at] = jnp.zeros(edge.shape[1:], F32)
            halo[side_at * HALO : (side_at + 1) * HALO] = jnp.zeros((HALO, *halo.shape[1:]), BF)

    at_last = places.spot // (places.plane - 1) * jnp.minimum(tiles - 1 - tile, 1)
    at_first = (places.plane - 1 - places.spot) // (places.plane - 1) * jnp.minimum(tile, 1)
    pl.semaphore_wait(barrier, places.groups + places.plane - 2 + at_last + at_first)

    def in_mem(at):
        return {"mem": at, "tile": tile}

    lat_copies = exchange(in_mem, mem, mems, lambda to: lat_ref, gathered, lat_sems)
    edge_copies = RowCopies(places, lambda s: edge_send.at[s], lambda s: edge.at[s], edge_sems)
    edge_copies.start()
    wells = Wells(cells_ref, count_ref, columns, picks, places, grid_cols, grid_cols * rows * tiles, rows)
    lines = layers * rows
    wells.fill(0, lines // 2)
    gathered[mem] = lat_ref[...]
    for copy in lat_copies:
        copy.wait()
    for s in range(mems):
        every_ref[share * s : share * (s + 1)] = gathered[s]
    for load in loads:
        load.wait()
    own_fields(every_ref[...], slab, left, own, mem, mems)
    send[0:HALO] = own[0:HALO].astype(BF)
    send[HALO : 2 * HALO] = own[rows - HALO : rows].astype(BF)
    halo_copies = RowCopies(
        places,
        lambda s: send.at[pl.ds(s * HALO, HALO)],
        lambda s: halo.at[pl.ds(s * HALO, HALO)],
        halo_sems,
    )
    halo_copies.start()
    own_windows(own, pieces)
    wells.fill(lines // 2, lines)
    edge_copies.wait()
    halo_copies.wait()
    all_windows(halo, pieces, windows, rows)
    convolve(windows, lift_w, mix_w, out_w, scale, (l0, l1, l2), (m0, m1), total, ends, tile, tiles, blocks)
    sweeps(
        own, halo, edge, prev_ref, source_ref, total, ends, perm, first, raw, values, mem, mems, tile, tiles
    )

    got = dot(values[...], picks[...])
    weight = got[0:members] + got[members : 2 * members]
    number = got[2 * members : 3 * members] + got[3 * members : 4 * members]
    low = iota((1, LANES), 1) < LANES // 2
    for t in range(places.groups // 2):
        n, w = number[:, t * LANES : (t + 1) * LANES], weight[:, t * LANES : (t + 1) * LANES]
        sums[2 * t] = jnp.where(low, n, pltpu.roll(w, LANES // 2, 1))
        sums[2 * t + 1] = jnp.where(low, pltpu.roll(n, LANES // 2, 1), w)

    def together(target):
        value = target[0]
        for at in range(1, target.shape[0]):
            value = value + target[at]
        return value

    group_copies = exchange(places.in_group, places.mine, places.groups, lambda to: sums.at[to], group_in, group_sems)
    group_in[places.mine] = sums[places.mine]
    for r in range(rows):
        for z in range(layers):
            press_ref[:, z, r, :] = raw[r, z * members : (z + 1) * members]
    for copy in group_copies:
        copy.wait()
    value = together(group_in)
    hold[0] = value
    plane_in[places.spot] = value
    plane_copies = exchange(places.in_plane, places.spot, places.plane, lambda to: hold.at[0], plane_in, plane_sems)
    for copy in plane_copies:
        copy.wait()
    value = together(plane_in)
    value = value / pltpu.roll(value, LANES // 2, 1)
    hold[1] = value
    data_ref[places.mine] = value
    data_copies = exchange(places.in_group, places.mine, places.groups, lambda to: hold.at[1], data_ref, data_sems)
    for copy in data_copies:
        copy.wait()


def main(latents, basis, prev, source, conv_in, conv_mid, conv_out, perf_cells, perf_count):
    share, latent = latents.shape
    mems, tiles = lax.axis_size("mem"), lax.axis_size("tile")
    members = share * mems
    _, layers, rows, width = basis.shape
    deep = layers * members
    channels = conv_in.shape[1]
    block = 4 * channels
    blocks = LANES // 2 + 2
    count = blocks // PER_WINDOW + 1
    out_rows = rows // 2 + 2
    slots = perf_cells.shape[1]
    plane = tiles // 2
    groups = 2 * mems
    lanes = groups // 2 * LANES
    vmem = pl.BlockSpec(memory_space=pltpu.VMEM)
    piece = (members, LANES)
    return pl.pallas_call(
        main_kernel,
        out_shape=[
            jax.ShapeDtypeStruct((members, layers, rows, LANES), F32),
            jax.ShapeDtypeStruct((members, latent), F32),
            jax.ShapeDtypeStruct((groups, *piece), F32),
        ],
        in_specs=[vmem, pl.BlockSpec(memory_space=pl.ANY)] + [vmem] * 7,
        out_specs=[vmem] * 3,
        scratch_shapes=[
            pltpu.VMEM((rows, deep, LANES), F32),
            pltpu.VMEM((mems, share, latent), F32),
            pltpu.VMEM((3, latent, layers, rows, LANES), BF),
            pltpu.VMEM((rows * members, latent * rows), BF),
            pltpu.VMEM((rows, deep, 2 * LANES), F32),
            pltpu.VMEM((2 * HALO, deep, 2 * LANES), BF),
            pltpu.VMEM((2 * HALO, deep, 2 * LANES), BF),
            pltpu.VMEM((2, 8, width), F32),
            pltpu.VMEM((2, 8, width), F32),
            pltpu.VMEM((16, channels), F32),
            pltpu.VMEM((PER_WINDOW + 4, block, block), BF),
            pltpu.VMEM((4 * block, block), BF),
            pltpu.VMEM((block, 2 * LANES), BF),
            pltpu.VMEM((1, block), F32),
            pltpu.VMEM((rows // 2 + HALO, count, deep, LANES), F32),
            pltpu.VMEM((count, out_rows + 1, deep, 2 * LANES), BF),
        ]
        + [pltpu.VMEM((2, (out_rows + 1) * deep, block), BF)] * 3
        + [pltpu.VMEM((2, out_rows * deep, block), BF)] * 2
        + [pltpu.VMEM((out_rows * deep, 2 * LANES), F32)] * 2
        + [pltpu.VMEM((rows + 4, 2, deep, LANES), F32)] * 2
        + [
            pltpu.VMEM((4 * members, layers * rows * LANES), BF),
            pltpu.VMEM((slots, LANES, lanes), BF),
            pltpu.VMEM((layers * rows * LANES, lanes), BF),
            pltpu.VMEM((groups, *piece), F32),
            pltpu.VMEM((groups, *piece), F32),
            pltpu.VMEM((plane, *piece), F32),
            pltpu.VMEM((2, *piece), F32),
            pltpu.SemaphoreType.DMA((3,)),
            pltpu.SemaphoreType.DMA((2, mems)),
            pltpu.SemaphoreType.DMA((2, 2)),
            pltpu.SemaphoreType.DMA((2, 2)),
            pltpu.SemaphoreType.DMA((2, groups)),
            pltpu.SemaphoreType.DMA((2, plane)),
            pltpu.SemaphoreType.DMA((2, groups)),
        ],
        compiler_params=pltpu.CompilerParams(collective_id=0, has_side_effects=True, vmem_limit_bytes=BIG),
        name="main",
    )(latents, basis, prev, source, conv_in, conv_mid, conv_out.reshape(1, channels), perf_cells.T,
      perf_count)


def update_kernel(
    pressure_ref, data_ref, every_ref, obs_ref, error_ref, press_ref, well_ref, new_ref, held, load_sem, store_sem
):
    load = pltpu.make_async_copy(pressure_ref, held, load_sem)
    load.start()
    mem, mems = lax.axis_index("mem"), lax.axis_size("mem")
    groups, members, _ = data_ref.shape
    each = obs_ref.shape[1] // groups
    lane = iota((1, LANES), 1)
    parts = []
    for t in range(obs_ref.shape[1] // LANES):
        part = jnp.zeros((members, LANES), F32)
        for g in range(groups):
            by = each * g - LANES * t
            if by <= -each or by >= LANES:
                continue
            moved = pltpu.roll(data_ref[g], by % LANES, 1)
            part = jnp.where((lane >= by) & (lane < by + each), moved, part)
        parts.append(part)
    wells = jnp.concatenate(parts, axis=1)
    well_ref[...] = wells
    scale = 2.0 * error_ref[...].reshape(1, -1)
    centred = wells - jnp.sum(wells, axis=0, keepdims=True) / members
    scaled = centred / (math.sqrt(members - 1) * scale)
    innov = (obs_ref[...] - wells) / scale
    exact = lax.Precision.HIGHEST
    eye = ones_where(iota((members, members), 0) == iota((members, members), 1))
    gram = eye + dot_nt(scaled, scaled, exact)
    cross = dot_nt(innov, scaled, exact)
    every = every_ref[...]
    spread = (every - jnp.sum(every, axis=0, keepdims=True) / members) / math.sqrt(members - 1)
    load.wait()
    store = pltpu.make_async_copy(held, press_ref, store_sem)
    store.start()
    columns = [jnp.broadcast_to(gram[:, j : j + 1], (members, LANES)) for j in range(members)]
    tiles = [spread[:, t * LANES : (t + 1) * LANES] for t in range(every.shape[1] // LANES)]
    row_at = iota((members, LANES), 0)
    for k in range(members):
        column = columns[k]
        inverse = 1.0 / column[k : k + 1]
        pivot_row = row_at == k

        def reduced(x):
            line = x[k : k + 1] * inverse
            return jnp.where(pivot_row, line, x - column * line)

        for j in range(k + 1, members):
            columns[j] = reduced(columns[j])
        tiles = [reduced(x) for x in tiles]
    solved = jnp.concatenate(tiles, axis=1)
    new = every + jnp.dot(cross, solved, preferred_element_type=F32, precision=exact)
    share = members // mems
    own = new[0:share]
    for s in range(1, mems):
        own = jnp.where(mem == s, new[s * share : (s + 1) * share], own)
    new_ref[...] = own
    store.wait()


def update(press, data, every, obs, error):
    _, members, _ = data.shape
    vmem = pl.BlockSpec(memory_space=pltpu.VMEM)
    held = pl.BlockSpec(memory_space=pl.ANY)
    return pl.pallas_call(
        update_kernel,
        out_shape=[
            jax.ShapeDtypeStruct(press.shape, F32),
            jax.ShapeDtypeStruct(obs.shape, F32),
            jax.ShapeDtypeStruct((members // lax.axis_size("mem"), every.shape[1]), F32),
        ],
        in_specs=[held] + [vmem] * 4,
        out_specs=[held] + [vmem] * 2,
        scratch_shapes=[pltpu.VMEM(press.shape, F32), pltpu.SemaphoreType.DMA(()), pltpu.SemaphoreType.DMA(())],
        name="update",
    )(press, data, every, obs, error)


def body(
    latents, basis, conv_in, conv_mid, conv_out, pressure_prev, source, perf_cells, perf_count, obs_perturbed, obs_error
):
    press, every, data = main(
        latents, basis, pressure_prev, source, conv_in, conv_mid, conv_out, perf_cells, perf_count
    )
    return tuple(update(press, data, every, obs_perturbed, obs_error))


def solution(mesh):
    return jax.shard_map(
        body,
        mesh=mesh,
        in_specs=(
            P("mem", None), P(None, None, "tile", None), P(), P(), P(), P(None, "tile", None), P(None, "tile", None),
            P(), P(), P(), P(),
        ),
        out_specs=(P(None, None, "tile", "mem"), P(), P("mem", None)),
        check_vma=False,
    )
```

```python
import math

import jax
import jax.numpy as jnp
from jax import lax
from jax.experimental import pallas as pl
from jax.experimental.pallas import tpu as pltpu
from jax.sharding import PartitionSpec as P

SWEEPS = 2
STORAGE = 1.0
BF = jnp.bfloat16
F32 = jnp.float32
LANES = 128
HALO = 4
WINDOW = 32
EARLY = 6
PER_WINDOW = (WINDOW - 2) // 2
MESH = pl.DeviceIdType.MESH
BIG = 60 * 2**20


def dot(a, b):
    return jnp.dot(a, b, preferred_element_type=F32)


def dot_nt(a, b, precision=None):
    return lax.dot_general(a, b, (((1,), (1,)), ((), ())), preferred_element_type=F32, precision=precision)


def iota(shape, axis):
    return lax.broadcasted_iota(jnp.int32, shape, axis)


def ones_where(cond):
    return jnp.where(cond, 1.0, 0.0)


class Places:
    def __init__(self, side):
        self.mem, self.tile = lax.axis_index("mem"), lax.axis_index("tile")
        self.mems, self.tiles = lax.axis_size("mem"), lax.axis_size("tile")
        self.side = side
        self.plane = side * side
        self.halves = self.tiles // self.plane
        self.groups = self.mems * self.halves
        self.mine = self.mem * self.halves + self.tile // self.plane
        self.spot = lax.rem(self.tile, self.plane)

    def in_group(self, g):
        return {"mem": g // self.halves, "tile": lax.rem(g, self.halves) * self.plane + self.spot}

    def in_plane(self, at):
        return {"mem": self.mem, "tile": self.tile // self.plane * self.plane + at}


def remote(source, target, sems, index, place):
    return pltpu.make_async_remote_copy(
        src_ref=source,
        dst_ref=target,
        send_sem=sems.at[0, index],
        recv_sem=sems.at[1, index],
        device_id=place,
        device_id_type=MESH,
    )


def exchange(place, at, size, source, target, sems):
    copies = []
    for step in range(1, size):
        to = lax.rem(at + step, size)
        copies.append(remote(source(to), target.at[at], sems, step, place(to)))
        copies[-1].start()
    return copies


class RowCopies:
    def __init__(self, places, source, target, sems):
        tile, last = places.tile, places.tiles - 1
        self.has = (tile > 0, tile < last)
        to = (jnp.maximum(tile - 1, 0), jnp.minimum(tile + 1, last))
        self.copies = [
            remote(source(side), target(1 - side), sems, side, {"mem": places.mem, "tile": to[side]})
            for side in range(2)
        ]

    def start(self):
        for side in range(2):
            pl.when(self.has[side])(self.copies[side].start)

    def wait(self):
        for side in range(2):
            pl.when(self.has[side])(self.copies[side].wait_send)
            pl.when(self.has[1 - side])(self.copies[side].wait_recv)


def own_fields(every, slab, left, own_ref, mem, mems):
    members, latent = every.shape
    rows = own_ref.shape[0]
    layers = slab.shape[2]
    every = every.astype(BF).astype(F32)
    groups = latent // rows
    wide = rows * rows
    group_of = iota((1, latent), 1) // rows
    picked = jnp.concatenate([every * ones_where(group_of == g) for g in range(groups)], axis=0).astype(BF)
    spread = ones_where(lax.rem(iota((latent, wide), 0), rows) == iota((latent, wide), 1) // rows).astype(BF)
    repeated = dot(picked, spread)
    lane_row = lax.rem(iota((1, wide), 1), rows)
    for g in range(groups):
        part = repeated[g * members : (g + 1) * members]
        stacked = jnp.concatenate([part * ones_where(lane_row == r) for r in range(rows)], axis=0)
        left[:, g * wide : (g + 1) * wide] = stacked.astype(BF)
    lane = iota((1, LANES), 1)
    keep_left = (ones_where(lane >= LANES // 2) * jnp.where(mem > 0, 1.0, 0.0)).astype(BF)
    keep_right = (ones_where(lane < LANES // 2) * jnp.where(mem < mems - 1, 1.0, 0.0)).astype(BF)
    for z in range(layers):
        own = slab[0, :, z].reshape(latent * rows, LANES)
        lhs = slab[1, :, z].reshape(latent * rows, LANES)
        rhs = slab[2, :, z].reshape(latent * rows, LANES)
        both = jnp.concatenate([own, lhs * keep_left + rhs * keep_right], axis=1)
        field = dot(left[...], both).reshape(rows, members, 2 * LANES)
        own_ref[:, z * members : (z + 1) * members] = field


def decoder_weights(conv_in_ref, conv_mid_ref, conv_out_ref, taps, lift_w, mix_w, out_w, scale, mem, mems, last):
    channels = conv_out_ref.shape[1]
    block = 4 * channels
    taps[...] = jnp.zeros_like(taps)
    taps[0:9] = conv_in_ref[...].astype(F32)
    repeat = ones_where(iota((channels, block), 0) == lax.rem(iota((channels, block), 1), channels)).astype(BF)
    in_rows = dot(taps[...].astype(BF), repeat)
    in_rows = jnp.concatenate([in_rows] * 4, axis=0)
    in_rows = (in_rows * ones_where(iota((64, block), 0) // 16 == iota((64, block), 1) // channels)).astype(BF)
    row = iota((block, 64), 0)
    col = iota((block, 64), 1)
    column = lax.rem(row, WINDOW)
    patch_row = lax.rem(row // WINDOW, 4)
    tap = lax.rem(col, 16)
    tap_row = jnp.where(tap >= 3, 1, 0) + jnp.where(tap >= 6, 1, 0)
    tap_col = tap - 3 * tap_row
    fits = (patch_row == col // 32 + tap_row) & (tap < 9)
    offset = jnp.where(fits, column - lax.rem(col // 16, 2) - tap_col, -1)
    col_of = lax.rem(iota((1, block), 1) // channels, 2)
    low, high = jnp.where(mem > 0, 1.0, 0.0), jnp.where(mem < mems - 1, 1.0, 0.0)
    for t in range(PER_WINDOW):
        weight = dot(ones_where(offset == 2 * t).astype(BF), in_rows)
        lift_w[t] = weight.astype(BF)
        if t == 0:
            lift_w[PER_WINDOW] = (weight * low).astype(BF)
        if t == 1:
            lift_w[PER_WINDOW + 1] = (weight * jnp.where(col_of == 0, low, 1.0)).astype(BF)
        if t == (last - 1) % PER_WINDOW:
            lift_w[PER_WINDOW + 2] = (weight * jnp.where(col_of == 1, high, 1.0)).astype(BF)
        if t == last % PER_WINDOW:
            lift_w[PER_WINDOW + 3] = (weight * high).astype(BF)
    mix_w[...] = jnp.zeros_like(mix_w)
    nothing = jnp.zeros((channels, channels), F32)
    for p in range(4):
        for q in range(4):
            at = ((q // 2) * 2 + p // 2) * block + ((p % 2) * 2 + q % 2) * channels
            for a in range(2):
                if not 0 <= p - a <= 2:
                    continue
                pair = [
                    conv_mid_ref[3 * (p - a) + q - b].astype(F32) if 0 <= q - b <= 2 else nothing for b in range(2)
                ]
                mix_w[at : at + channels, a * 2 * channels : (a + 1) * 2 * channels] = (
                    jnp.concatenate(pair, axis=0).T.astype(BF)
                )
    out_row = conv_out_ref[...].astype(F32)
    scale[...] = jnp.concatenate([out_row] * 4, axis=1)
    row = iota((block, 2 * LANES), 0)
    lane = iota((block, 2 * LANES), 1)
    match = (row // LANES == lane // LANES) & (lax.rem(row // (LANES // 2), 2) == lax.rem(lane, 2))
    match = match & (lax.rem(row // (LANES // 4), 2) == lax.rem(lane // (LANES // 2), 2))
    out_w[...] = ones_where(match).astype(BF)


def pair_pieces(pieces, q, even, odd):
    lane = iota((1, LANES), 1)
    count = pieces.shape[1]

    def row_pieces(field, odd):
        own, halo = field[:, :LANES], field[:, LANES:]
        low = jnp.where(lane < LANES // 2, own, halo)
        high = jnp.where(lane < LANES // 2, halo, own)
        out = []
        for w in range(count):
            start = (WINDOW - 2) * w - HALO
            from_tile = low if w == 0 else high if w == count - 1 else own
            out.append(pltpu.roll(from_tile, (WINDOW * odd - start) % LANES, 1))
        return out

    evens, odds = row_pieces(even, 0), row_pieces(odd, 1)
    for w in range(count):
        pieces[q, w] = jnp.where(lane < WINDOW, evens[w], odds[w])


def own_windows(own_ref, pieces):
    def own_pair(q, carry):
        pair_pieces(pieces, q + HALO // 2, own_ref[2 * q], own_ref[2 * q + 1])
        return carry

    lax.fori_loop(0, own_ref.shape[0] // 2, own_pair, 0)


def halo_windows(halo_ref, pieces, rows):
    for half in range(HALO // 2):
        pair_pieces(pieces, half, halo_ref[2 * half].astype(F32), halo_ref[2 * half + 1].astype(F32))
        at = HALO + 2 * half
        pair_pieces(pieces, (rows + at) // 2, halo_ref[at].astype(F32), halo_ref[at + 1].astype(F32))


def fill_windows(pieces, windows, begin, end):
    lane = iota((1, LANES), 1)

    def block_row(i, carry):
        for w in range(windows.shape[0]):
            both = jnp.where(lane < LANES // 2, pieces[i, w], pltpu.roll(pieces[i + 1, w], LANES // 2, 1))
            high = both.astype(BF)
            windows[w, i] = jnp.concatenate([high, (both - high.astype(F32)).astype(BF)], axis=1)
        return carry

    lax.fori_loop(begin, end, block_row, 0)


def decoder(windows, lift_w, mix_w, out_w, scale, lifted, mixed, total, ends, tile, tiles, blocks):
    count, block_rows, deep, _ = windows.shape
    size = (block_rows - 1) * deep
    lane = iota((1, 2 * LANES), 1)
    half = lax.rem(lane, LANES // 2)
    part = lane // LANES
    top = jnp.where(tile > 0, 1.0, 0.0)
    bottom = jnp.where(tile < tiles - 1, 1.0, 0.0)
    masks = {
        0: jnp.zeros((1, 2 * LANES), F32) + top,
        1: jnp.where(part == 0, top, 1.0),
        block_rows - 2: jnp.where(part == 1, bottom, 1.0),
        block_rows - 1: jnp.zeros((1, 2 * LANES), F32) + bottom,
    }
    steps = (blocks - 2) // 2
    streams = (lambda t: 1 + t, lambda t: 1 + steps + t)
    keep = [ones_where(half < LANES // 4).astype(BF), ones_where(half >= LANES // 4).astype(BF)]

    def stack(values):
        return values[0] if len(values) == 1 else jnp.concatenate(values, axis=0)

    def lift(places, slot, spans):
        for u in range(2):
            at = places[u]
            if isinstance(at, int) and at in (0, 1, blocks - 1, blocks):
                w, index = at // PER_WINDOW, PER_WINDOW + (0, 1, blocks - 1, blocks).index(at)
            else:
                at = jnp.minimum(at, blocks)
                w = at // PER_WINDOW
                index = at - w * PER_WINDOW
                for special, j in ((2, blocks - 1), (3, blocks)):
                    index = jnp.where(at == j, PER_WINDOW + special, index)
            lhs = stack([windows[w, i : i + n + 1].reshape((n + 1) * deep, -1) for i, n in spans])
            value = jnp.maximum(dot(lhs, lift_w[index]), 0.0)
            done = 0
            for first, n in spans:
                parts = []
                for i in range(first, first + n + 1):
                    part = value[done : done + deep]
                    parts.append(part * masks[i] if i in masks else part)
                    done += deep
                lifted[slot][u, first * deep : (first + n + 1) * deep] = stack(parts).astype(BF)

    def mix(slot, to, spans):
        operands = []
        for u in range(2):
            x, y = lifted[slot].at[u], lifted[(slot + 1) % 3].at[u]
            for i, n in spans:
                here, below = slice(i * deep, (i + n) * deep), slice((i + 1) * deep, (i + n + 1) * deep)
                operands.append(jnp.concatenate([x[here], x[below], y[here], y[below]], axis=1))
        each = len(spans)
        for u in range(2):
            if each == 1:
                value = dot(operands[u], mix_w[...])
            else:
                if u == 0:
                    joined = dot(stack(operands), mix_w[...])
                rows = joined.shape[0] // 2
                value = joined[u * rows : (u + 1) * rows]
            value = jnp.maximum(value, 0.0) * scale[...]
            by = LANES - LANES // 4 if u == 0 else LANES // 4
            other = [pltpu.roll(value[:, i * LANES : (i + 1) * LANES], by, 1) for i in range(2)]
            value = (value + jnp.concatenate(other, axis=1)).astype(BF)
            done = 0
            for i, n in spans:
                mixed[to][u, i * deep : (i + n) * deep] = value[done : done + n * deep]
                done += n * deep

    def both_streams(at, spans):
        parts = [mixed[at][0, i * deep : (i + n) * deep] * keep[0] + mixed[at][1, i * deep : (i + n) * deep] * keep[1]
                 for i, n in spans]
        return dot(stack(parts), out_w[...])

    def contract(t, at, spans):
        value = both_streams(at, spans)
        done = 0
        for i, n in spans:
            rows = slice(i * deep, (i + n) * deep)
            total[rows] = jnp.where(half // 2 == t, value[done : done + n * deep], total[rows])
            done += n * deep

    def ahead(t):
        return [stream(t) for stream in streams]

    def run(begin, end, spans, last=()):
        lift(ahead(begin), 0, spans)
        lift(ahead(begin + 1), 1, spans)
        mix(0, 0, spans)
        lift(ahead(begin + 2), 2, spans)
        whole = (end - begin - 2) // 6

        def body(q, carry):
            for v in range(6):
                t = begin + 1 + q * 6 + v
                contract(t - 1, v % 2, spans)
                mix((1 + v) % 3, (1 + v) % 2, spans)
                lift(ahead(t + 2), v % 3, spans)
            return carry

        if whole:
            lax.fori_loop(0, whole, body, 0)
        for step in range(1 + 6 * whole, end - begin):
            contract(begin + step - 1, (step - 1) % 2, spans)
            mix(step % 3, step % 2, spans)
            if step < end - begin - 1:
                lift(ahead(begin + step + 2), (step + 2) % 3, spans)
        final = end - begin - 1
        if last:
            lift((0, blocks - 1), (final + 2) % 3, last)
            lift((1, blocks), final % 3, last)
            mix((final + 2) % 3, (final + 1) % 2, last)
        contract(end - 1, final % 2, spans)
        if last:
            value = both_streams((final + 1) % 2, last)
            swapped = [pltpu.roll(value[:, i * LANES : (i + 1) * LANES], LANES // 2, 1) for i in range(2)]
            ends[...] = jnp.concatenate(swapped, axis=1)

    return run, steps


def sweeps(
    own_ref, halo_ref, edge_ref, prev_ref, source_ref, total, ends, perm, first, press_ref, values,
    mem, mems, tile, tiles,
):
    rows = own_ref.shape[0]
    deep = own_ref.shape[1]
    layers = prev_ref.shape[0]
    members = deep // layers
    lane = iota((1, LANES), 1)
    top = jnp.where(tile > 0, 1.0, 0.0)
    bottom = jnp.where(tile < tiles - 1, 1.0, 0.0)
    beyond = jnp.where(lane < LANES // 2, jnp.where(mem < mems - 1, 1.0, 0.0), jnp.where(mem > 0, 1.0, 0.0))
    mine = pl.multiple_of(mem * LANES, LANES)
    before = pl.multiple_of(jnp.maximum(mem - 1, 0) * LANES, LANES)
    after = pl.multiple_of(jnp.minimum(mem + 1, mems - 1) * LANES, LANES)

    def columns(line):
        beside = jnp.where(lane < LANES // 2, line(after), line(before))
        return line(mine), beside

    def levels(pick):
        each = [columns(lambda at: pick(z, at)) for z in range(layers)]
        return [
            jnp.concatenate([jnp.broadcast_to(each[z][t], (members, LANES)) for z in range(layers)], axis=0)
            for t in range(2)
        ]

    def prev_line(index):
        r = index - 2
        if r < 0:
            return levels(lambda z, at: edge_ref[0, 2 * z + 2 + r : 2 * z + 3 + r, pl.ds(at, LANES)])
        if r >= rows:
            return levels(lambda z, at: edge_ref[1, 2 * z + r - rows : 2 * z + r - rows + 1, pl.ds(at, LANES)])
        return levels(lambda z, at: prev_ref[z, r : r + 1, pl.ds(at, LANES)])

    def source_line(index):
        r = index - 2
        if r < 0:
            return levels(lambda z, at: edge_ref[0, 4 + z : 5 + z, pl.ds(at, LANES)])
        if r >= rows:
            return levels(lambda z, at: edge_ref[1, 4 + z : 5 + z, pl.ds(at, LANES)])
        return levels(lambda z, at: source_ref[z, r : r + 1, pl.ds(at, LANES)])

    for index in range(rows + 4):
        r = index - 2
        i, a = index // 2, index % 2
        for t, parts in enumerate((total, ends)):
            value = parts[i * deep : (i + 1) * deep, a * LANES : (a + 1) * LANES]
            if 0 <= r < rows:
                field = own_ref[r, :, t * LANES : (t + 1) * LANES]
            else:
                at = HALO + r if r < 0 else HALO + r - rows
                field = halo_ref[at, :, t * LANES : (t + 1) * LANES].astype(F32)
            value = jnp.exp(field + value)
            if r < 0:
                value = jnp.where(top > 0, value, 0.0)
            if r >= rows:
                value = jnp.where(bottom > 0, value, 0.0)
            if t == 1:
                value = jnp.where(beyond > 0, value, 0.0)
            perm[index, t] = value

    def shift(own, beside, by):
        edge = LANES - 1 if by > 0 else 0
        a, b = pltpu.roll(own, -by % LANES, 1), pltpu.roll(beside, -by % LANES, 1)
        return jnp.where(lane == edge, b, a), jnp.where(lane == edge, a, b)

    def harmonic(a, b):
        both = a + b
        return jnp.where(both > 0, 2.0 * a * b / jnp.where(both > 0, both, 1.0), 0.0)

    def swap(x):
        return jnp.concatenate([x[members:], x[:members]], axis=0)

    def coefficients(index):
        here = [perm[index, t] for t in range(2)]
        right = shift(here[0], here[1], 1)
        across = [harmonic(here[t], right[t]) for t in range(2)]
        back = shift(across[0], across[1], -1)
        out = []
        for t in range(2):
            level = harmonic(here[t][:members], here[t][members:])
            out.append((across[t], back[t], jnp.concatenate([level, level], axis=0)))
        return out

    up = [harmonic(perm[0, t], perm[1, t]) for t in range(2)]
    for index in range(1, rows + 3):
        over, here, under = prev_line(index - 1), prev_line(index), prev_line(index + 1)
        down = [harmonic(perm[index, t], perm[index + 1, t]) for t in range(2)]
        coef = coefficients(index)
        right, back = shift(here[0], here[1], 1), shift(here[0], here[1], -1)
        source = source_line(index)
        for t in range(2):
            east, west, level = coef[t]
            acc = STORAGE * here[t] + source[t]
            acc = acc + down[t] * under[t] + up[t] * over[t]
            acc = acc + east * right[t] + west * back[t] + level * swap(here[t])
            first[index, t] = acc / (STORAGE + down[t] + up[t] + east + west + level)
        up = down
    up = harmonic(perm[1, 0], perm[2, 0])
    for index in range(2, rows + 2):
        r = index - 2
        down = harmonic(perm[index, 0], perm[index + 1, 0])
        east, west, level = coefficients(index)[0]
        here = first[index, 0]
        right = shift(here, first[index, 1], 1)[0]
        back = shift(here, first[index, 1], -1)[0]
        acc = STORAGE * prev_line(index)[0] + source_line(index)[0]
        acc = acc + down * first[index + 1, 0] + up * first[index - 1, 0]
        acc = acc + east * right + west * back + level * swap(here)
        press = acc / (STORAGE + down + up + east + west + level)
        up = down
        k = perm[index, 0]
        press_ref[r] = press
        for z in range(layers):
            level_press = press[z * members : (z + 1) * members]
            level_perm = k[z * members : (z + 1) * members]
            at = (z * rows + r) * LANES
            for q, value in enumerate((level_perm, level_perm * level_press)):
                high = value.astype(BF).astype(F32)
                both = jnp.concatenate([high, value - high], axis=0).astype(BF)
                values[2 * q * members : 2 * (q + 1) * members, at : at + LANES] = both


class Wells:
    def __init__(self, cells_ref, count_ref, columns, picks, places, grid_cols, grid_cells, rows):
        slots, wells = cells_ref.shape
        each = wells // places.groups
        half = LANES // 2
        ids = cells_ref[...]
        ids = jnp.where(iota((slots, wells), 0) < count_ref[...].reshape(1, wells), ids, -1)
        layer = ids // grid_cells
        rest = ids - layer * grid_cells
        row = rest // grid_cols
        col = rest - row * grid_cols - places.mem * LANES
        row = row - places.tile * rows
        inside = (ids >= 0) & (row >= 0) & (row < rows) & (col >= 0) & (col < LANES)
        code = jnp.where(inside, (layer * rows + row) * LANES + col, -1)
        lane = iota((1, LANES), 1)
        tiles = []
        for t in range(places.groups // 2):
            tile = jnp.full((slots, LANES), -1, jnp.int32)
            for g in (2 * t, 2 * t + 1):
                to = half * (g % 2)
                for source in range(wells // LANES):
                    by = to - (each * g - LANES * source)
                    low, high = max(to, by), min(to + each, by + LANES)
                    if low < high:
                        moved = pltpu.roll(code[:, source * LANES : (source + 1) * LANES], by % LANES, 1)
                        tile = jnp.where((lane >= low) & (lane < high), moved, tile)
            tiles.append(tile)
        code = jnp.concatenate(tiles, axis=1)
        self.line = jnp.where(code >= 0, code // LANES, -1)
        column = jnp.where(code >= 0, lax.rem(code, LANES), -1)
        for slot in range(slots):
            columns[slot] = ones_where(iota((LANES, 1), 0) == column[slot : slot + 1]).astype(BF)
        self.columns, self.picks = columns, picks

    def fill(self, begin, end):
        slots = self.columns.shape[0]

        def each(line, carry):
            here = ones_where(self.line == line).astype(BF)
            value = self.columns[0] * here[0:1]
            for slot in range(1, slots):
                value = value + self.columns[slot] * here[slot : slot + 1]
            self.picks[pl.ds(pl.multiple_of(line * LANES, LANES), LANES)] = value
            return carry

        lax.fori_loop(begin, end, each, 0)


def main_kernel(
    lat_ref, basis_ref, prev_ref, source_ref, conv_in_ref, conv_mid_ref, conv_out_ref, cells_ref, count_ref,
    press_ref, every_ref, data_ref,
    raw, gathered, slab, left, own, halo, send, edge, edge_send,
    taps, lift_w, mix_w, out_w, scale, pieces, windows, l0, l1, l2, m0, m1, total, ends, perm, first, values,
    columns, picks, sums, group_in, plane_in, hold,
    slab_sems, lat_sems, edge_sems, halo_sems, group_sems, plane_sems, data_sems,
):
    side = math.isqrt(plane_in.shape[0])
    places = Places(side)
    mem, mems, tile, tiles = places.mem, places.mems, places.tile, places.tiles
    share = lat_ref.shape[0]
    members = share * mems
    layers, rows, grid_cols = prev_ref.shape
    blocks = LANES // 2 + 2

    loads = []
    for part, offset in enumerate((0, -1, 1)):
        at = jnp.clip(mem + offset, 0, mems - 1)
        loads.append(
            pltpu.make_async_copy(
                basis_ref.at[:, :, :, pl.ds(pl.multiple_of(at * LANES, LANES), LANES)],
                slab.at[part],
                slab_sems.at[part],
            )
        )
    for load in loads:
        load.start()

    barrier = pltpu.get_barrier_semaphore()
    for step in range(1, places.groups):
        to = places.in_group(lax.rem(places.mine + step, places.groups))
        pl.semaphore_signal(barrier, inc=1, device_id=to, device_id_type=MESH)
    for step in range(1, places.plane):
        to = places.in_plane(lax.rem(places.spot + step, places.plane))
        pl.semaphore_signal(barrier, inc=1, device_id=to, device_id_type=MESH)
    for ends_at, to in ((places.plane - 1, tile + 1), (0, tile - 1)):

        @pl.when((places.spot == ends_at) & (to >= 0) & (to < tiles))
        def _(to=to):
            pl.semaphore_signal(barrier, inc=1, device_id={"mem": mem, "tile": to}, device_id_type=MESH)

    decoder_weights(conv_in_ref, conv_mid_ref, conv_out_ref, taps, lift_w, mix_w, out_w, scale, mem, mems, blocks)
    for side_at in range(2):
        begin = 0 if side_at == 0 else rows - 2
        at = 0 if side_at == 0 else rows - 1
        for z in range(layers):
            edge_send[side_at, 2 * z : 2 * z + 2] = prev_ref[z, begin : begin + 2]
            edge_send[side_at, 4 + z : 5 + z] = source_ref[z, at : at + 1]
        edge_send[side_at, 6:8] = jnp.zeros((2, grid_cols), F32)
    for side_at, at_end in ((0, tile == 0), (1, tile == tiles - 1)):

        @pl.when(at_end)
        def _(side_at=side_at):
            edge[side_at] = jnp.zeros(edge.shape[1:], F32)
            halo[side_at * HALO : (side_at + 1) * HALO] = jnp.zeros((HALO, *halo.shape[1:]), BF)

    at_last = places.spot // (places.plane - 1) * jnp.minimum(tiles - 1 - tile, 1)
    at_first = (places.plane - 1 - places.spot) // (places.plane - 1) * jnp.minimum(tile, 1)
    pl.semaphore_wait(barrier, places.groups + places.plane - 2 + at_last + at_first)

    def in_mem(at):
        return {"mem": at, "tile": tile}

    lat_copies = exchange(in_mem, mem, mems, lambda to: lat_ref, gathered, lat_sems)
    edge_copies = RowCopies(places, lambda s: edge_send.at[s], lambda s: edge.at[s], edge_sems)
    edge_copies.start()
    wells = Wells(cells_ref, count_ref, columns, picks, places, grid_cols, grid_cols * rows * tiles, rows)
    lines = layers * rows
    wells.fill(0, lines)
    gathered[mem] = lat_ref[...]
    for copy in lat_copies:
        copy.wait()
    for s in range(mems):
        every_ref[share * s : share * (s + 1)] = gathered[s]
    for load in loads:
        load.wait()
    own_fields(every_ref[...], slab, left, own, mem, mems)
    send[0:HALO] = own[0:HALO].astype(BF)
    send[HALO : 2 * HALO] = own[rows - HALO : rows].astype(BF)
    halo_copies = RowCopies(
        places,
        lambda s: send.at[pl.ds(s * HALO, HALO)],
        lambda s: halo.at[pl.ds(s * HALO, HALO)],
        halo_sems,
    )
    halo_copies.start()
    own_windows(own, pieces)
    inner = HALO // 2
    outer = rows // 2 + inner
    fill_windows(pieces, windows, inner, outer - 1)
    run, steps = decoder(
        windows, lift_w, mix_w, out_w, scale, (l0, l1, l2), (m0, m1), total, ends, tile, tiles, blocks
    )
    total[...] = jnp.zeros_like(total)
    run(0, EARLY, ((inner, rows // 2 - 2),))
    edge_copies.wait()
    halo_copies.wait()
    halo_windows(halo, pieces, rows)
    fill_windows(pieces, windows, 0, inner)
    fill_windows(pieces, windows, outer - 1, outer + 1)
    run(0, EARLY, ((0, inner), (outer - 2, inner)))
    run(EARLY, steps, ((0, outer),), last=((0, outer),))
    sweeps(
        own, halo, edge, prev_ref, source_ref, total, ends, perm, first, raw, values, mem, mems, tile, tiles
    )

    got = dot(values[...], picks[...])
    weight = got[0:members] + got[members : 2 * members]
    number = got[2 * members : 3 * members] + got[3 * members : 4 * members]
    low = iota((1, LANES), 1) < LANES // 2
    for t in range(places.groups // 2):
        n, w = number[:, t * LANES : (t + 1) * LANES], weight[:, t * LANES : (t + 1) * LANES]
        sums[2 * t] = jnp.where(low, n, pltpu.roll(w, LANES // 2, 1))
        sums[2 * t + 1] = jnp.where(low, pltpu.roll(n, LANES // 2, 1), w)

    def together(target):
        value = target[0]
        for at in range(1, target.shape[0]):
            value = value + target[at]
        return value

    group_copies = exchange(places.in_group, places.mine, places.groups, lambda to: sums.at[to], group_in, group_sems)
    group_in[places.mine] = sums[places.mine]
    for r in range(rows):
        for z in range(layers):
            press_ref[:, z, r, :] = raw[r, z * members : (z + 1) * members]
    for copy in group_copies:
        copy.wait()
    value = together(group_in)
    hold[0] = value
    plane_in[places.spot] = value
    plane_copies = exchange(places.in_plane, places.spot, places.plane, lambda to: hold.at[0], plane_in, plane_sems)
    for copy in plane_copies:
        copy.wait()
    value = together(plane_in)
    value = value / pltpu.roll(value, LANES // 2, 1)
    hold[1] = value
    data_ref[places.mine] = value
    data_copies = exchange(places.in_group, places.mine, places.groups, lambda to: hold.at[1], data_ref, data_sems)
    for copy in data_copies:
        copy.wait()


def main(latents, basis, prev, source, conv_in, conv_mid, conv_out, perf_cells, perf_count):
    share, latent = latents.shape
    mems, tiles = lax.axis_size("mem"), lax.axis_size("tile")
    members = share * mems
    _, layers, rows, width = basis.shape
    deep = layers * members
    channels = conv_in.shape[1]
    block = 4 * channels
    blocks = LANES // 2 + 2
    count = blocks // PER_WINDOW + 1
    out_rows = rows // 2 + 2
    slots = perf_cells.shape[1]
    plane = tiles // 2
    groups = 2 * mems
    lanes = groups // 2 * LANES
    vmem = pl.BlockSpec(memory_space=pltpu.VMEM)
    piece = (members, LANES)
    return pl.pallas_call(
        main_kernel,
        out_shape=[
            jax.ShapeDtypeStruct((members, layers, rows, LANES), F32),
            jax.ShapeDtypeStruct((members, latent), F32),
            jax.ShapeDtypeStruct((groups, *piece), F32),
        ],
        in_specs=[vmem, pl.BlockSpec(memory_space=pl.ANY)] + [vmem] * 7,
        out_specs=[vmem] * 3,
        scratch_shapes=[
            pltpu.VMEM((rows, deep, LANES), F32),
            pltpu.VMEM((mems, share, latent), F32),
            pltpu.VMEM((3, latent, layers, rows, LANES), BF),
            pltpu.VMEM((rows * members, latent * rows), BF),
            pltpu.VMEM((rows, deep, 2 * LANES), F32),
            pltpu.VMEM((2 * HALO, deep, 2 * LANES), BF),
            pltpu.VMEM((2 * HALO, deep, 2 * LANES), BF),
            pltpu.VMEM((2, 8, width), F32),
            pltpu.VMEM((2, 8, width), F32),
            pltpu.VMEM((16, channels), F32),
            pltpu.VMEM((PER_WINDOW + 4, block, block), BF),
            pltpu.VMEM((4 * block, block), BF),
            pltpu.VMEM((block, 2 * LANES), BF),
            pltpu.VMEM((1, block), F32),
            pltpu.VMEM((rows // 2 + HALO, count, deep, LANES), F32),
            pltpu.VMEM((count, out_rows + 1, deep, 2 * LANES), BF),
        ]
        + [pltpu.VMEM((2, (out_rows + 1) * deep, block), BF)] * 3
        + [pltpu.VMEM((2, out_rows * deep, block), BF)] * 2
        + [pltpu.VMEM((out_rows * deep, 2 * LANES), F32)] * 2
        + [pltpu.VMEM((rows + 4, 2, deep, LANES), F32)] * 2
        + [
            pltpu.VMEM((4 * members, layers * rows * LANES), BF),
            pltpu.VMEM((slots, LANES, lanes), BF),
            pltpu.VMEM((layers * rows * LANES, lanes), BF),
            pltpu.VMEM((groups, *piece), F32),
            pltpu.VMEM((groups, *piece), F32),
            pltpu.VMEM((plane, *piece), F32),
            pltpu.VMEM((2, *piece), F32),
            pltpu.SemaphoreType.DMA((3,)),
            pltpu.SemaphoreType.DMA((2, mems)),
            pltpu.SemaphoreType.DMA((2, 2)),
            pltpu.SemaphoreType.DMA((2, 2)),
            pltpu.SemaphoreType.DMA((2, groups)),
            pltpu.SemaphoreType.DMA((2, plane)),
            pltpu.SemaphoreType.DMA((2, groups)),
        ],
        compiler_params=pltpu.CompilerParams(collective_id=0, has_side_effects=True, vmem_limit_bytes=BIG),
        name="main",
    )(latents, basis, prev, source, conv_in, conv_mid, conv_out.reshape(1, channels), perf_cells.T,
      perf_count)


def update_kernel(
    pressure_ref, data_ref, every_ref, obs_ref, error_ref, press_ref, well_ref, new_ref, held, load_sem, store_sem
):
    load = pltpu.make_async_copy(pressure_ref, held, load_sem)
    load.start()
    mem, mems = lax.axis_index("mem"), lax.axis_size("mem")
    groups, members, _ = data_ref.shape
    each = obs_ref.shape[1] // groups
    lane = iota((1, LANES), 1)
    parts = []
    for t in range(obs_ref.shape[1] // LANES):
        part = jnp.zeros((members, LANES), F32)
        for g in range(groups):
            by = each * g - LANES * t
            if by <= -each or by >= LANES:
                continue
            moved = pltpu.roll(data_ref[g], by % LANES, 1)
            part = jnp.where((lane >= by) & (lane < by + each), moved, part)
        parts.append(part)
    wells = jnp.concatenate(parts, axis=1)
    well_ref[...] = wells
    scale = 2.0 * error_ref[...].reshape(1, -1)
    centred = wells - jnp.sum(wells, axis=0, keepdims=True) / members
    scaled = centred / (math.sqrt(members - 1) * scale)
    innov = (obs_ref[...] - wells) / scale
    exact = lax.Precision.HIGHEST
    eye = ones_where(iota((members, members), 0) == iota((members, members), 1))
    gram = eye + dot_nt(scaled, scaled, exact)
    cross = dot_nt(innov, scaled, exact)
    every = every_ref[...]
    spread = (every - jnp.sum(every, axis=0, keepdims=True) / members) / math.sqrt(members - 1)
    load.wait()
    store = pltpu.make_async_copy(held, press_ref, store_sem)
    store.start()
    columns = [jnp.broadcast_to(gram[:, j : j + 1], (members, LANES)) for j in range(members)]
    tiles = [spread[:, t * LANES : (t + 1) * LANES] for t in range(every.shape[1] // LANES)]
    row_at = iota((members, LANES), 0)
    for k in range(members):
        column = columns[k]
        inverse = 1.0 / column[k : k + 1]
        pivot_row = row_at == k

        def reduced(x):
            line = x[k : k + 1] * inverse
            return jnp.where(pivot_row, line, x - column * line)

        for j in range(k + 1, members):
            columns[j] = reduced(columns[j])
        tiles = [reduced(x) for x in tiles]
    solved = jnp.concatenate(tiles, axis=1)
    new = every + jnp.dot(cross, solved, preferred_element_type=F32, precision=exact)
    share = members // mems
    own = new[0:share]
    for s in range(1, mems):
        own = jnp.where(mem == s, new[s * share : (s + 1) * share], own)
    new_ref[...] = own
    store.wait()


def update(press, data, every, obs, error):
    _, members, _ = data.shape
    vmem = pl.BlockSpec(memory_space=pltpu.VMEM)
    held = pl.BlockSpec(memory_space=pl.ANY)
    return pl.pallas_call(
        update_kernel,
        out_shape=[
            jax.ShapeDtypeStruct(press.shape, F32),
            jax.ShapeDtypeStruct(obs.shape, F32),
            jax.ShapeDtypeStruct((members // lax.axis_size("mem"), every.shape[1]), F32),
        ],
        in_specs=[held] + [vmem] * 4,
        out_specs=[held] + [vmem] * 2,
        scratch_shapes=[pltpu.VMEM(press.shape, F32), pltpu.SemaphoreType.DMA(()), pltpu.SemaphoreType.DMA(())],
        name="update",
    )(press, data, every, obs, error)


def body(
    latents, basis, conv_in, conv_mid, conv_out, pressure_prev, source, perf_cells, perf_count, obs_perturbed, obs_error
):
    press, every, data = main(
        latents, basis, pressure_prev, source, conv_in, conv_mid, conv_out, perf_cells, perf_count
    )
    return tuple(update(press, data, every, obs_perturbed, obs_error))


def solution(mesh):
    return jax.shard_map(
        body,
        mesh=mesh,
        in_specs=(
            P("mem", None), P(None, None, "tile", None), P(), P(), P(), P(None, "tile", None), P(None, "tile", None),
            P(), P(), P(), P(),
        ),
        out_specs=(P(None, None, "tile", "mem"), P(), P("mem", None)),
        check_vma=False,
    )
```

```python
import math

import jax
import jax.numpy as jnp
from jax import lax
from jax.experimental import pallas as pl
from jax.experimental.pallas import tpu as pltpu
from jax.sharding import PartitionSpec as P

SWEEPS = 2
STORAGE = 1.0
BF = jnp.bfloat16
F32 = jnp.float32
LANES = 128
HALO = 4
WINDOW = 32
EARLY = 4
PER_WINDOW = (WINDOW - 2) // 2
MESH = pl.DeviceIdType.MESH
BIG = 60 * 2**20
TINY = 2.0**-126


def dot(a, b):
    return jnp.dot(a, b, preferred_element_type=F32)


def dot_nt(a, b, precision=None):
    return lax.dot_general(a, b, (((1,), (1,)), ((), ())), preferred_element_type=F32, precision=precision)


def iota(shape, axis):
    return lax.broadcasted_iota(jnp.int32, shape, axis)


def ones_where(cond):
    return jnp.where(cond, 1.0, 0.0)


class Places:
    def __init__(self, side):
        self.mem, self.tile = lax.axis_index("mem"), lax.axis_index("tile")
        self.mems, self.tiles = lax.axis_size("mem"), lax.axis_size("tile")
        self.side = side
        self.plane = side * side
        self.halves = self.tiles // self.plane
        self.groups = self.mems * self.halves
        self.mine = self.mem * self.halves + self.tile // self.plane
        self.spot = lax.rem(self.tile, self.plane)

    def in_group(self, g):
        return {"mem": g // self.halves, "tile": lax.rem(g, self.halves) * self.plane + self.spot}

    def in_plane(self, at):
        return {"mem": self.mem, "tile": self.tile // self.plane * self.plane + at}


def remote(source, target, sems, index, place):
    return pltpu.make_async_remote_copy(
        src_ref=source,
        dst_ref=target,
        send_sem=sems.at[0, index],
        recv_sem=sems.at[1, index],
        device_id=place,
        device_id_type=MESH,
    )


def exchange(place, at, size, source, target, sems):
    copies = []
    for step in range(1, size):
        to = lax.rem(at + step, size)
        copies.append(remote(source(to), target.at[at], sems, step, place(to)))
        copies[-1].start()
    return copies


class RowCopies:
    def __init__(self, places, source, target, sems):
        tile, last = places.tile, places.tiles - 1
        self.has = (tile > 0, tile < last)
        to = (jnp.maximum(tile - 1, 0), jnp.minimum(tile + 1, last))
        self.copies = [
            remote(source(side), target(1 - side), sems, side, {"mem": places.mem, "tile": to[side]})
            for side in range(2)
        ]

    def start(self):
        for side in range(2):
            pl.when(self.has[side])(self.copies[side].start)

    def wait(self):
        for side in range(2):
            pl.when(self.has[side])(self.copies[side].wait_send)
            pl.when(self.has[1 - side])(self.copies[side].wait_recv)


def own_fields(every, slab, left, own_ref, mem, mems):
    members, latent = every.shape
    rows = own_ref.shape[0]
    layers = slab.shape[2]
    every = every.astype(BF).astype(F32)
    groups = latent // rows
    wide = rows * rows
    group_of = iota((1, latent), 1) // rows
    picked = jnp.concatenate([every * ones_where(group_of == g) for g in range(groups)], axis=0).astype(BF)
    spread = ones_where(lax.rem(iota((latent, wide), 0), rows) == iota((latent, wide), 1) // rows).astype(BF)
    repeated = dot(picked, spread)
    lane_row = lax.rem(iota((1, wide), 1), rows)
    for g in range(groups):
        part = repeated[g * members : (g + 1) * members]
        stacked = jnp.concatenate([part * ones_where(lane_row == r) for r in range(rows)], axis=0)
        left[:, g * wide : (g + 1) * wide] = stacked.astype(BF)
    lane = iota((1, LANES), 1)
    keep_left = (ones_where(lane >= LANES // 2) * jnp.where(mem > 0, 1.0, 0.0)).astype(BF)
    keep_right = (ones_where(lane < LANES // 2) * jnp.where(mem < mems - 1, 1.0, 0.0)).astype(BF)
    for z in range(layers):
        own = slab[0, :, z].reshape(latent * rows, LANES)
        lhs = slab[1, :, z].reshape(latent * rows, LANES)
        rhs = slab[2, :, z].reshape(latent * rows, LANES)
        both = jnp.concatenate([own, lhs * keep_left + rhs * keep_right], axis=1)
        field = dot(left[...], both).reshape(rows, members, 2 * LANES)
        own_ref[:, z * members : (z + 1) * members] = field


def decoder_weights(conv_in_ref, conv_mid_ref, conv_out_ref, taps, lift_w, mix_w, out_w, scale, mem, mems, last):
    channels = conv_out_ref.shape[1]
    block = 4 * channels
    taps[...] = jnp.zeros_like(taps)
    taps[0:9] = conv_in_ref[...].astype(F32)
    repeat = ones_where(iota((channels, block), 0) == lax.rem(iota((channels, block), 1), channels)).astype(BF)
    in_rows = dot(taps[...].astype(BF), repeat)
    in_rows = jnp.concatenate([in_rows] * 4, axis=0)
    in_rows = (in_rows * ones_where(iota((64, block), 0) // 16 == iota((64, block), 1) // channels)).astype(BF)
    row = iota((block, 64), 0)
    col = iota((block, 64), 1)
    column = lax.rem(row, WINDOW)
    patch_row = lax.rem(row // WINDOW, 4)
    tap = lax.rem(col, 16)
    tap_row = jnp.where(tap >= 3, 1, 0) + jnp.where(tap >= 6, 1, 0)
    tap_col = tap - 3 * tap_row
    fits = (patch_row == col // 32 + tap_row) & (tap < 9)
    offset = jnp.where(fits, column - lax.rem(col // 16, 2) - tap_col, -1)
    col_of = lax.rem(iota((1, block), 1) // channels, 2)
    low, high = jnp.where(mem > 0, 1.0, 0.0), jnp.where(mem < mems - 1, 1.0, 0.0)
    for t in range(PER_WINDOW):
        weight = dot(ones_where(offset == 2 * t).astype(BF), in_rows)
        lift_w[t] = weight.astype(BF)
        if t == 0:
            lift_w[PER_WINDOW] = (weight * low).astype(BF)
        if t == 1:
            lift_w[PER_WINDOW + 1] = (weight * jnp.where(col_of == 0, low, 1.0)).astype(BF)
        if t == (last - 1) % PER_WINDOW:
            lift_w[PER_WINDOW + 2] = (weight * jnp.where(col_of == 1, high, 1.0)).astype(BF)
        if t == last % PER_WINDOW:
            lift_w[PER_WINDOW + 3] = (weight * high).astype(BF)
    mix_w[...] = jnp.zeros_like(mix_w)
    nothing = jnp.zeros((channels, channels), F32)
    for p in range(4):
        for q in range(4):
            at = ((q // 2) * 2 + p // 2) * block + ((p % 2) * 2 + q % 2) * channels
            for a in range(2):
                if not 0 <= p - a <= 2:
                    continue
                pair = [
                    conv_mid_ref[3 * (p - a) + q - b].astype(F32) if 0 <= q - b <= 2 else nothing for b in range(2)
                ]
                mix_w[at : at + channels, a * 2 * channels : (a + 1) * 2 * channels] = (
                    jnp.concatenate(pair, axis=0).T.astype(BF)
                )
    out_row = conv_out_ref[...].astype(F32)
    scale[...] = jnp.concatenate([out_row] * 4, axis=1)
    row = iota((block, 2 * LANES), 0)
    lane = iota((block, 2 * LANES), 1)
    match = (row // LANES == lane // LANES) & (lax.rem(row // (LANES // 2), 2) == lax.rem(lane, 2))
    match = match & (lax.rem(row // (LANES // 4), 2) == lax.rem(lane // (LANES // 2), 2))
    out_w[...] = ones_where(match).astype(BF)


def pair_pieces(pieces, q, even, odd):
    lane = iota((1, LANES), 1)
    count = pieces.shape[1]

    def row_pieces(field, odd):
        own, halo = field[:, :LANES], field[:, LANES:]
        low = jnp.where(lane < LANES // 2, own, halo)
        high = jnp.where(lane < LANES // 2, halo, own)
        out = []
        for w in range(count):
            start = (WINDOW - 2) * w - HALO
            from_tile = low if w == 0 else high if w == count - 1 else own
            out.append(pltpu.roll(from_tile, (WINDOW * odd - start) % LANES, 1))
        return out

    evens, odds = row_pieces(even, 0), row_pieces(odd, 1)
    for w in range(count):
        pieces[q, w] = jnp.where(lane < WINDOW, evens[w], odds[w])


def own_windows(own_ref, pieces):
    def own_pair(q, carry):
        pair_pieces(pieces, q + HALO // 2, own_ref[2 * q], own_ref[2 * q + 1])
        return carry

    lax.fori_loop(0, own_ref.shape[0] // 2, own_pair, 0)


def halo_windows(halo_ref, pieces, rows):
    for half in range(HALO // 2):
        pair_pieces(pieces, half, halo_ref[2 * half].astype(F32), halo_ref[2 * half + 1].astype(F32))
        at = HALO + 2 * half
        pair_pieces(pieces, (rows + at) // 2, halo_ref[at].astype(F32), halo_ref[at + 1].astype(F32))


def fill_windows(pieces, windows, begin, end):
    lane = iota((1, LANES), 1)

    def block_row(i, carry):
        for w in range(windows.shape[0]):
            both = jnp.where(lane < LANES // 2, pieces[i, w], pltpu.roll(pieces[i + 1, w], LANES // 2, 1))
            high = both.astype(BF)
            windows[w, i] = jnp.concatenate([high, (both - high.astype(F32)).astype(BF)], axis=1)
        return carry

    lax.fori_loop(begin, end, block_row, 0)


def decoder(windows, lift_w, mix_w, out_w, scale, lifted, mixed, total, ends, tile, tiles, blocks):
    count, block_rows, deep, _ = windows.shape
    size = (block_rows - 1) * deep
    lane = iota((1, 2 * LANES), 1)
    half = lax.rem(lane, LANES // 2)
    part = lane // LANES
    top = jnp.where(tile > 0, 1.0, 0.0)
    bottom = jnp.where(tile < tiles - 1, 1.0, 0.0)
    masks = {
        0: jnp.zeros((1, 2 * LANES), F32) + top,
        1: jnp.where(part == 0, top, 1.0),
        block_rows - 2: jnp.where(part == 1, bottom, 1.0),
        block_rows - 1: jnp.zeros((1, 2 * LANES), F32) + bottom,
    }
    steps = (blocks - 2) // 2
    streams = (lambda t: 1 + t, lambda t: 1 + steps + t)
    keep = [ones_where(half < LANES // 4).astype(BF), ones_where(half >= LANES // 4).astype(BF)]

    def stack(values):
        return values[0] if len(values) == 1 else jnp.concatenate(values, axis=0)

    def lift(places, slot, spans):
        for u in range(2):
            at = places[u]
            if isinstance(at, int) and at in (0, 1, blocks - 1, blocks):
                w, index = at // PER_WINDOW, PER_WINDOW + (0, 1, blocks - 1, blocks).index(at)
            else:
                at = jnp.minimum(at, blocks)
                w = at // PER_WINDOW
                index = at - w * PER_WINDOW
                for special, j in ((2, blocks - 1), (3, blocks)):
                    index = jnp.where(at == j, PER_WINDOW + special, index)
            lhs = stack([windows[w, i : i + n + 1].reshape((n + 1) * deep, -1) for i, n in spans])
            value = jnp.maximum(dot(lhs, lift_w[index]), 0.0)
            done = 0
            for first, n in spans:
                parts = []
                for i in range(first, first + n + 1):
                    part = value[done : done + deep]
                    parts.append(part * masks[i] if i in masks else part)
                    done += deep
                lifted[slot][u, first * deep : (first + n + 1) * deep] = stack(parts).astype(BF)

    def mix(slot, to, spans):
        operands = []
        for u in range(2):
            x, y = lifted[slot].at[u], lifted[(slot + 1) % 3].at[u]
            for i, n in spans:
                here, below = slice(i * deep, (i + n) * deep), slice((i + 1) * deep, (i + n + 1) * deep)
                operands.append(jnp.concatenate([x[here], x[below], y[here], y[below]], axis=1))
        each = len(spans)
        for u in range(2):
            if each == 1:
                value = dot(operands[u], mix_w[...])
            else:
                if u == 0:
                    joined = dot(stack(operands), mix_w[...])
                rows = joined.shape[0] // 2
                value = joined[u * rows : (u + 1) * rows]
            value = jnp.maximum(value, 0.0) * scale[...]
            by = LANES - LANES // 4 if u == 0 else LANES // 4
            other = [pltpu.roll(value[:, i * LANES : (i + 1) * LANES], by, 1) for i in range(2)]
            value = (value + jnp.concatenate(other, axis=1)).astype(BF)
            done = 0
            for i, n in spans:
                mixed[to][u, i * deep : (i + n) * deep] = value[done : done + n * deep]
                done += n * deep

    def both_streams(at, spans):
        parts = [mixed[at][0, i * deep : (i + n) * deep] * keep[0] + mixed[at][1, i * deep : (i + n) * deep] * keep[1]
                 for i, n in spans]
        return dot(stack(parts), out_w[...])

    def contract(t, at, spans):
        value = both_streams(at, spans)
        done = 0
        for i, n in spans:
            rows = slice(i * deep, (i + n) * deep)
            total[rows] = jnp.where(half // 2 == t, value[done : done + n * deep], total[rows])
            done += n * deep

    def ahead(t):
        return [stream(t) for stream in streams]

    def run(begin, end, spans, last=()):
        lift(ahead(begin), 0, spans)
        lift(ahead(begin + 1), 1, spans)
        mix(0, 0, spans)
        lift(ahead(begin + 2), 2, spans)
        whole = (end - begin - 2) // 6

        def body(q, carry):
            for v in range(6):
                t = begin + 1 + q * 6 + v
                contract(t - 1, v % 2, spans)
                mix((1 + v) % 3, (1 + v) % 2, spans)
                lift(ahead(t + 2), v % 3, spans)
            return carry

        if whole:
            lax.fori_loop(0, whole, body, 0)
        for step in range(1 + 6 * whole, end - begin):
            contract(begin + step - 1, (step - 1) % 2, spans)
            mix(step % 3, step % 2, spans)
            if step < end - begin - 1:
                lift(ahead(begin + step + 2), (step + 2) % 3, spans)
        final = end - begin - 1
        if last:
            lift((0, blocks - 1), (final + 2) % 3, last)
            lift((1, blocks), final % 3, last)
            mix((final + 2) % 3, (final + 1) % 2, last)
        contract(end - 1, final % 2, spans)
        if last:
            value = both_streams((final + 1) % 2, last)
            swapped = [pltpu.roll(value[:, i * LANES : (i + 1) * LANES], LANES // 2, 1) for i in range(2)]
            ends[...] = jnp.concatenate(swapped, axis=1)

    return run, steps


def sweeps(
    own_ref, halo_ref, edge_ref, prev_ref, source_ref, total, ends, perm, first, press_ref, values,
    mem, mems, tile, tiles,
):
    rows = own_ref.shape[0]
    deep = own_ref.shape[1]
    layers = prev_ref.shape[0]
    members = deep // layers
    lane = iota((1, LANES), 1)
    top = jnp.where(tile > 0, 1.0, 0.0)
    bottom = jnp.where(tile < tiles - 1, 1.0, 0.0)
    beyond = jnp.where(lane < LANES // 2, jnp.where(mem < mems - 1, 1.0, 0.0), jnp.where(mem > 0, 1.0, 0.0))
    mine = pl.multiple_of(mem * LANES, LANES)
    before = pl.multiple_of(jnp.maximum(mem - 1, 0) * LANES, LANES)
    after = pl.multiple_of(jnp.minimum(mem + 1, mems - 1) * LANES, LANES)

    def columns(line):
        beside = jnp.where(lane < LANES // 2, line(after), line(before))
        return line(mine), beside

    def levels(pick):
        each = [columns(lambda at: pick(z, at)) for z in range(layers)]
        return [
            jnp.concatenate([jnp.broadcast_to(each[z][t], (members, LANES)) for z in range(layers)], axis=0)
            for t in range(2)
        ]

    def prev_line(index):
        r = index - 2
        if r < 0:
            return levels(lambda z, at: edge_ref[0, 2 * z + 2 + r : 2 * z + 3 + r, pl.ds(at, LANES)])
        if r >= rows:
            return levels(lambda z, at: edge_ref[1, 2 * z + r - rows : 2 * z + r - rows + 1, pl.ds(at, LANES)])
        return levels(lambda z, at: prev_ref[z, r : r + 1, pl.ds(at, LANES)])

    def source_line(index):
        r = index - 2
        if r < 0:
            return levels(lambda z, at: edge_ref[0, 4 + z : 5 + z, pl.ds(at, LANES)])
        if r >= rows:
            return levels(lambda z, at: edge_ref[1, 4 + z : 5 + z, pl.ds(at, LANES)])
        return levels(lambda z, at: source_ref[z, r : r + 1, pl.ds(at, LANES)])

    for index in range(rows + 4):
        r = index - 2
        i, a = index // 2, index % 2
        for t, parts in enumerate((total, ends)):
            value = parts[i * deep : (i + 1) * deep, a * LANES : (a + 1) * LANES]
            if 0 <= r < rows:
                field = own_ref[r, :, t * LANES : (t + 1) * LANES]
            else:
                at = HALO + r if r < 0 else HALO + r - rows
                field = halo_ref[at, :, t * LANES : (t + 1) * LANES].astype(F32)
            value = jnp.exp(field + value)
            if r < 0:
                value = jnp.where(top > 0, value, 0.0)
            if r >= rows:
                value = jnp.where(bottom > 0, value, 0.0)
            if t == 1:
                value = jnp.where(beyond > 0, value, 0.0)
            perm[index, t] = value

    def shift(own, beside, by):
        edge = LANES - 1 if by > 0 else 0
        a, b = pltpu.roll(own, -by % LANES, 1), pltpu.roll(beside, -by % LANES, 1)
        return jnp.where(lane == edge, b, a), jnp.where(lane == edge, a, b)

    def harmonic(a, b):
        return 2.0 * a * b / jnp.maximum(a + b, TINY)

    def swap(x):
        return jnp.concatenate([x[members:], x[:members]], axis=0)

    def coefficients(index):
        here = [perm[index, t] for t in range(2)]
        right = shift(here[0], here[1], 1)
        across = [harmonic(here[t], right[t]) for t in range(2)]
        back = shift(across[0], across[1], -1)
        out = []
        for t in range(2):
            level = harmonic(here[t][:members], here[t][members:])
            out.append((across[t], back[t], jnp.concatenate([level, level], axis=0)))
        return out

    up = [harmonic(perm[0, t], perm[1, t]) for t in range(2)]
    for index in range(1, rows + 3):
        over, here, under = prev_line(index - 1), prev_line(index), prev_line(index + 1)
        down = [harmonic(perm[index, t], perm[index + 1, t]) for t in range(2)]
        coef = coefficients(index)
        right, back = shift(here[0], here[1], 1), shift(here[0], here[1], -1)
        source = source_line(index)
        for t in range(2 if 2 <= index < rows + 2 else 1):
            east, west, level = coef[t]
            acc = STORAGE * here[t] + source[t]
            acc = acc + down[t] * under[t] + up[t] * over[t]
            acc = acc + east * right[t] + west * back[t] + level * swap(here[t])
            first[index, t] = acc / (STORAGE + down[t] + up[t] + east + west + level)
        up = down
    up = harmonic(perm[1, 0], perm[2, 0])
    for index in range(2, rows + 2):
        r = index - 2
        down = harmonic(perm[index, 0], perm[index + 1, 0])
        east, west, level = coefficients(index)[0]
        here = first[index, 0]
        right = shift(here, first[index, 1], 1)[0]
        back = shift(here, first[index, 1], -1)[0]
        acc = STORAGE * prev_line(index)[0] + source_line(index)[0]
        acc = acc + down * first[index + 1, 0] + up * first[index - 1, 0]
        acc = acc + east * right + west * back + level * swap(here)
        press = acc / (STORAGE + down + up + east + west + level)
        up = down
        k = perm[index, 0]
        press_ref[r] = press
        for z in range(layers):
            level_press = press[z * members : (z + 1) * members]
            level_perm = k[z * members : (z + 1) * members]
            at = (z * rows + r) * LANES
            for q, value in enumerate((level_perm, level_perm * level_press)):
                high = value.astype(BF).astype(F32)
                both = jnp.concatenate([high, value - high], axis=0).astype(BF)
                values[2 * q * members : 2 * (q + 1) * members, at : at + LANES] = both


class Wells:
    def __init__(self, cells_ref, count_ref, columns, picks, places, grid_cols, grid_cells, rows):
        slots, wells = cells_ref.shape
        each = wells // places.groups
        half = LANES // 2
        ids = cells_ref[...]
        ids = jnp.where(iota((slots, wells), 0) < count_ref[...].reshape(1, wells), ids, -1)
        layer = ids // grid_cells
        rest = ids - layer * grid_cells
        row = rest // grid_cols
        col = rest - row * grid_cols - places.mem * LANES
        row = row - places.tile * rows
        inside = (ids >= 0) & (row >= 0) & (row < rows) & (col >= 0) & (col < LANES)
        code = jnp.where(inside, (layer * rows + row) * LANES + col, -1)
        lane = iota((1, LANES), 1)
        tiles = []
        for t in range(places.groups // 2):
            tile = jnp.full((slots, LANES), -1, jnp.int32)
            for g in (2 * t, 2 * t + 1):
                to = half * (g % 2)
                for source in range(wells // LANES):
                    by = to - (each * g - LANES * source)
                    low, high = max(to, by), min(to + each, by + LANES)
                    if low < high:
                        moved = pltpu.roll(code[:, source * LANES : (source + 1) * LANES], by % LANES, 1)
                        tile = jnp.where((lane >= low) & (lane < high), moved, tile)
            tiles.append(tile)
        code = jnp.concatenate(tiles, axis=1)
        self.line = jnp.where(code >= 0, code // LANES, -1)
        column = jnp.where(code >= 0, lax.rem(code, LANES), -1)
        for slot in range(slots):
            columns[slot] = ones_where(iota((LANES, 1), 0) == column[slot : slot + 1]).astype(BF)
        self.columns, self.picks = columns, picks

    def fill(self, begin, end):
        slots = self.columns.shape[0]

        def each(line, carry):
            here = ones_where(self.line == line).astype(BF)
            value = self.columns[0] * here[0:1]
            for slot in range(1, slots):
                value = value + self.columns[slot] * here[slot : slot + 1]
            self.picks[pl.ds(pl.multiple_of(line * LANES, LANES), LANES)] = value
            return carry

        lax.fori_loop(begin, end, each, 0)


def main_kernel(
    lat_ref, basis_ref, prev_ref, source_ref, conv_in_ref, conv_mid_ref, conv_out_ref, cells_ref, count_ref,
    press_ref, every_ref, data_ref,
    raw, gathered, slab, left, own, halo, send, edge, edge_send,
    taps, lift_w, mix_w, out_w, scale, pieces, windows, l0, l1, l2, m0, m1, total, ends, perm, first, values,
    columns, picks, sums, group_in, plane_in, hold,
    slab_sems, lat_sems, edge_sems, halo_sems, group_sems, plane_sems, data_sems,
):
    side = math.isqrt(plane_in.shape[0])
    places = Places(side)
    mem, mems, tile, tiles = places.mem, places.mems, places.tile, places.tiles
    share = lat_ref.shape[0]
    members = share * mems
    layers, rows, grid_cols = prev_ref.shape
    blocks = LANES // 2 + 2

    loads = []
    for part, offset in enumerate((0, -1, 1)):
        at = jnp.clip(mem + offset, 0, mems - 1)
        loads.append(
            pltpu.make_async_copy(
                basis_ref.at[:, :, :, pl.ds(pl.multiple_of(at * LANES, LANES), LANES)],
                slab.at[part],
                slab_sems.at[part],
            )
        )
    for load in loads:
        load.start()

    barrier = pltpu.get_barrier_semaphore()
    for step in range(1, places.groups):
        to = places.in_group(lax.rem(places.mine + step, places.groups))
        pl.semaphore_signal(barrier, inc=1, device_id=to, device_id_type=MESH)
    for step in range(1, places.plane):
        to = places.in_plane(lax.rem(places.spot + step, places.plane))
        pl.semaphore_signal(barrier, inc=1, device_id=to, device_id_type=MESH)
    for ends_at, to in ((places.plane - 1, tile + 1), (0, tile - 1)):

        @pl.when((places.spot == ends_at) & (to >= 0) & (to < tiles))
        def _(to=to):
            pl.semaphore_signal(barrier, inc=1, device_id={"mem": mem, "tile": to}, device_id_type=MESH)

    decoder_weights(conv_in_ref, conv_mid_ref, conv_out_ref, taps, lift_w, mix_w, out_w, scale, mem, mems, blocks)
    for side_at in range(2):
        begin = 0 if side_at == 0 else rows - 2
        at = 0 if side_at == 0 else rows - 1
        for z in range(layers):
            edge_send[side_at, 2 * z : 2 * z + 2] = prev_ref[z, begin : begin + 2]
            edge_send[side_at, 4 + z : 5 + z] = source_ref[z, at : at + 1]
        edge_send[side_at, 6:8] = jnp.zeros((2, grid_cols), F32)
    for side_at, at_end in ((0, tile == 0), (1, tile == tiles - 1)):

        @pl.when(at_end)
        def _(side_at=side_at):
            edge[side_at] = jnp.zeros(edge.shape[1:], F32)
            halo[side_at * HALO : (side_at + 1) * HALO] = jnp.zeros((HALO, *halo.shape[1:]), BF)

    at_last = places.spot // (places.plane - 1) * jnp.minimum(tiles - 1 - tile, 1)
    at_first = (places.plane - 1 - places.spot) // (places.plane - 1) * jnp.minimum(tile, 1)
    pl.semaphore_wait(barrier, places.groups + places.plane - 2 + at_last + at_first)

    def in_mem(at):
        return {"mem": at, "tile": tile}

    lat_copies = exchange(in_mem, mem, mems, lambda to: lat_ref, gathered, lat_sems)
    edge_copies = RowCopies(places, lambda s: edge_send.at[s], lambda s: edge.at[s], edge_sems)
    edge_copies.start()
    wells = Wells(cells_ref, count_ref, columns, picks, places, grid_cols, grid_cols * rows * tiles, rows)
    lines = layers * rows
    wells.fill(0, lines)
    gathered[mem] = lat_ref[...]
    for copy in lat_copies:
        copy.wait()
    for s in range(mems):
        every_ref[share * s : share * (s + 1)] = gathered[s]
    for load in loads:
        load.wait()
    own_fields(every_ref[...], slab, left, own, mem, mems)
    send[0:HALO] = own[0:HALO].astype(BF)
    send[HALO : 2 * HALO] = own[rows - HALO : rows].astype(BF)
    halo_copies = RowCopies(
        places,
        lambda s: send.at[pl.ds(s * HALO, HALO)],
        lambda s: halo.at[pl.ds(s * HALO, HALO)],
        halo_sems,
    )
    halo_copies.start()
    own_windows(own, pieces)
    inner = HALO // 2
    outer = rows // 2 + inner
    fill_windows(pieces, windows, inner, outer - 1)
    run, steps = decoder(
        windows, lift_w, mix_w, out_w, scale, (l0, l1, l2), (m0, m1), total, ends, tile, tiles, blocks
    )
    total[...] = jnp.zeros_like(total)
    run(0, EARLY, ((inner, rows // 2 - 2),))
    edge_copies.wait()
    halo_copies.wait()
    halo_windows(halo, pieces, rows)
    fill_windows(pieces, windows, 0, inner)
    fill_windows(pieces, windows, outer - 1, outer + 1)
    run(0, EARLY, ((0, inner), (outer - 2, inner)))
    run(EARLY, steps, ((0, outer),), last=((0, outer),))
    sweeps(
        own, halo, edge, prev_ref, source_ref, total, ends, perm, first, raw, values, mem, mems, tile, tiles
    )

    got = dot(values[...], picks[...])
    weight = got[0:members] + got[members : 2 * members]
    number = got[2 * members : 3 * members] + got[3 * members : 4 * members]
    low = iota((1, LANES), 1) < LANES // 2
    for t in range(places.groups // 2):
        n, w = number[:, t * LANES : (t + 1) * LANES], weight[:, t * LANES : (t + 1) * LANES]
        sums[2 * t] = jnp.where(low, n, pltpu.roll(w, LANES // 2, 1))
        sums[2 * t + 1] = jnp.where(low, pltpu.roll(n, LANES // 2, 1), w)

    def together(target):
        value = target[0]
        for at in range(1, target.shape[0]):
            value = value + target[at]
        return value

    group_copies = exchange(places.in_group, places.mine, places.groups, lambda to: sums.at[to], group_in, group_sems)
    group_in[places.mine] = sums[places.mine]
    for r in range(rows):
        for z in range(layers):
            press_ref[:, z, r, :] = raw[r, z * members : (z + 1) * members]
    for copy in group_copies:
        copy.wait()
    value = together(group_in)
    hold[0] = value
    plane_in[places.spot] = value
    plane_copies = exchange(places.in_plane, places.spot, places.plane, lambda to: hold.at[0], plane_in, plane_sems)
    for copy in plane_copies:
        copy.wait()
    value = together(plane_in)
    value = value / pltpu.roll(value, LANES // 2, 1)
    hold[1] = value
    data_ref[places.mine] = value
    data_copies = exchange(places.in_group, places.mine, places.groups, lambda to: hold.at[1], data_ref, data_sems)
    for copy in data_copies:
        copy.wait()


def main(latents, basis, prev, source, conv_in, conv_mid, conv_out, perf_cells, perf_count):
    share, latent = latents.shape
    mems, tiles = lax.axis_size("mem"), lax.axis_size("tile")
    members = share * mems
    _, layers, rows, width = basis.shape
    deep = layers * members
    channels = conv_in.shape[1]
    block = 4 * channels
    blocks = LANES // 2 + 2
    count = blocks // PER_WINDOW + 1
    out_rows = rows // 2 + 2
    slots = perf_cells.shape[1]
    plane = tiles // 2
    groups = 2 * mems
    lanes = groups // 2 * LANES
    vmem = pl.BlockSpec(memory_space=pltpu.VMEM)
    piece = (members, LANES)
    return pl.pallas_call(
        main_kernel,
        out_shape=[
            jax.ShapeDtypeStruct((members, layers, rows, LANES), F32),
            jax.ShapeDtypeStruct((members, latent), F32),
            jax.ShapeDtypeStruct((groups, *piece), F32),
        ],
        in_specs=[vmem, pl.BlockSpec(memory_space=pl.ANY)] + [vmem] * 7,
        out_specs=[vmem] * 3,
        scratch_shapes=[
            pltpu.VMEM((rows, deep, LANES), F32),
            pltpu.VMEM((mems, share, latent), F32),
            pltpu.VMEM((3, latent, layers, rows, LANES), BF),
            pltpu.VMEM((rows * members, latent * rows), BF),
            pltpu.VMEM((rows, deep, 2 * LANES), F32),
            pltpu.VMEM((2 * HALO, deep, 2 * LANES), BF),
            pltpu.VMEM((2 * HALO, deep, 2 * LANES), BF),
            pltpu.VMEM((2, 8, width), F32),
            pltpu.VMEM((2, 8, width), F32),
            pltpu.VMEM((16, channels), F32),
            pltpu.VMEM((PER_WINDOW + 4, block, block), BF),
            pltpu.VMEM((4 * block, block), BF),
            pltpu.VMEM((block, 2 * LANES), BF),
            pltpu.VMEM((1, block), F32),
            pltpu.VMEM((rows // 2 + HALO, count, deep, LANES), F32),
            pltpu.VMEM((count, out_rows + 1, deep, 2 * LANES), BF),
        ]
        + [pltpu.VMEM((2, (out_rows + 1) * deep, block), BF)] * 3
        + [pltpu.VMEM((2, out_rows * deep, block), BF)] * 2
        + [pltpu.VMEM((out_rows * deep, 2 * LANES), F32)] * 2
        + [pltpu.VMEM((rows + 4, 2, deep, LANES), F32)] * 2
        + [
            pltpu.VMEM((4 * members, layers * rows * LANES), BF),
            pltpu.VMEM((slots, LANES, lanes), BF),
            pltpu.VMEM((layers * rows * LANES, lanes), BF),
            pltpu.VMEM((groups, *piece), F32),
            pltpu.VMEM((groups, *piece), F32),
            pltpu.VMEM((plane, *piece), F32),
            pltpu.VMEM((2, *piece), F32),
            pltpu.SemaphoreType.DMA((3,)),
            pltpu.SemaphoreType.DMA((2, mems)),
            pltpu.SemaphoreType.DMA((2, 2)),
            pltpu.SemaphoreType.DMA((2, 2)),
            pltpu.SemaphoreType.DMA((2, groups)),
            pltpu.SemaphoreType.DMA((2, plane)),
            pltpu.SemaphoreType.DMA((2, groups)),
        ],
        compiler_params=pltpu.CompilerParams(collective_id=0, has_side_effects=True, vmem_limit_bytes=BIG),
        name="main",
    )(latents, basis, prev, source, conv_in, conv_mid, conv_out.reshape(1, channels), perf_cells.T,
      perf_count)


def update_kernel(
    pressure_ref, data_ref, every_ref, obs_ref, error_ref, press_ref, well_ref, new_ref, held, load_sem, store_sem
):
    load = pltpu.make_async_copy(pressure_ref, held, load_sem)
    load.start()
    mem, mems = lax.axis_index("mem"), lax.axis_size("mem")
    groups, members, _ = data_ref.shape
    each = obs_ref.shape[1] // groups
    lane = iota((1, LANES), 1)
    parts = []
    for t in range(obs_ref.shape[1] // LANES):
        part = jnp.zeros((members, LANES), F32)
        for g in range(groups):
            by = each * g - LANES * t
            if by <= -each or by >= LANES:
                continue
            moved = pltpu.roll(data_ref[g], by % LANES, 1)
            part = jnp.where((lane >= by) & (lane < by + each), moved, part)
        parts.append(part)
    wells = jnp.concatenate(parts, axis=1)
    well_ref[...] = wells
    scale = 2.0 * error_ref[...].reshape(1, -1)
    centred = wells - jnp.sum(wells, axis=0, keepdims=True) / members
    scaled = centred / (math.sqrt(members - 1) * scale)
    innov = (obs_ref[...] - wells) / scale
    exact = lax.Precision.HIGHEST
    eye = ones_where(iota((members, members), 0) == iota((members, members), 1))
    gram = eye + dot_nt(scaled, scaled, exact)
    cross = dot_nt(innov, scaled, exact)
    every = every_ref[...]
    spread = (every - jnp.sum(every, axis=0, keepdims=True) / members) / math.sqrt(members - 1)
    load.wait()
    store = pltpu.make_async_copy(held, press_ref, store_sem)
    store.start()
    columns = [jnp.broadcast_to(gram[:, j : j + 1], (members, LANES)) for j in range(members)]
    tiles = [spread[:, t * LANES : (t + 1) * LANES] for t in range(every.shape[1] // LANES)]
    row_at = iota((members, LANES), 0)
    for k in range(members):
        column = columns[k]
        inverse = 1.0 / column[k : k + 1]
        pivot_row = row_at == k

        def reduced(x):
            line = x[k : k + 1] * inverse
            return jnp.where(pivot_row, line, x - column * line)

        for j in range(k + 1, members):
            columns[j] = reduced(columns[j])
        tiles = [reduced(x) for x in tiles]
    solved = jnp.concatenate(tiles, axis=1)
    new = every + jnp.dot(cross, solved, preferred_element_type=F32, precision=exact)
    share = members // mems
    own = new[0:share]
    for s in range(1, mems):
        own = jnp.where(mem == s, new[s * share : (s + 1) * share], own)
    new_ref[...] = own
    store.wait()


def update(press, data, every, obs, error):
    _, members, _ = data.shape
    vmem = pl.BlockSpec(memory_space=pltpu.VMEM)
    held = pl.BlockSpec(memory_space=pl.ANY)
    return pl.pallas_call(
        update_kernel,
        out_shape=[
            jax.ShapeDtypeStruct(press.shape, F32),
            jax.ShapeDtypeStruct(obs.shape, F32),
            jax.ShapeDtypeStruct((members // lax.axis_size("mem"), every.shape[1]), F32),
        ],
        in_specs=[held] + [vmem] * 4,
        out_specs=[held] + [vmem] * 2,
        scratch_shapes=[pltpu.VMEM(press.shape, F32), pltpu.SemaphoreType.DMA(()), pltpu.SemaphoreType.DMA(())],
        name="update",
    )(press, data, every, obs, error)


def body(
    latents, basis, conv_in, conv_mid, conv_out, pressure_prev, source, perf_cells, perf_count, obs_perturbed, obs_error
):
    press, every, data = main(
        latents, basis, pressure_prev, source, conv_in, conv_mid, conv_out, perf_cells, perf_count
    )
    return tuple(update(press, data, every, obs_perturbed, obs_error))


def solution(mesh):
    return jax.shard_map(
        body,
        mesh=mesh,
        in_specs=(
            P("mem", None), P(None, None, "tile", None), P(), P(), P(), P(None, "tile", None), P(None, "tile", None),
            P(), P(), P(), P(),
        ),
        out_specs=(P(None, None, "tile", "mem"), P(), P("mem", None)),
        check_vma=False,
    )
```
